32 devices in a mesh: span: 4 (over y, x), tensor: 8 (over z, core).
Axes of the slice: x: 2, y: 2, z: 4, core: 2. Of those that a mesh axis runs over, the one named last changes fastest.
Arguments:
- tokens: bfloat16 [1024, 4096], P('span', 'tensor'), may hold values from -200 to 200
- retain: float32 [1024], P('span'), may hold values from 0.5 to 1
- norm_gain: float32 [4096], P('tensor'), may hold values from 0.1 to 1.9
- norm_bias: float32 [4096], P('tensor'), may hold values from -2.5 to 2.5
- decay_rate: float32 [16, 4096], P(None, 'tensor'), may hold values from 0.00024414062 to 0.0333333333
- ema_angle: float32 [16, 4096], P(None, 'tensor'), may hold values from -0.05 to 0.05
- ema_input: float32 [16, 4096], P(None, 'tensor'), may hold values from -2.4 to 2.4
- ema_output: float32 [2, 16, 4096], P(None, None, 'tensor'), may hold values from -0.25 to 0.25
- ema_skip: float32 [4096], P('tensor'), may hold values from -3 to 3
- shared_weight: bfloat16 [4096, 1024], P('tensor'), may hold values from -0.125 to 0.125
- shared_gain: float32 [1024], replicated, may hold values from 0.1 to 1.9
- output_weight: bfloat16 [1024, 4096], P(None, 'tensor'), may hold values from -0.1875 to 0.1875
Outputs:
- layer_out: bfloat16 [1024, 4096], P('span', 'tensor')
The draws below stay inside these ranges and needn't reach their ends.
All inputs are finite; a program needn't handle non-finite values.
Results may differ from the reference program's by a relative error of at most 0.02.
Values may be sent and summed in bfloat16 or wider, within the bound.
A program may use at most 128 MiB of HBM per device.

```python
import jax
import jax.numpy as jnp
from jax import lax

D = 4096
NDIM = 16
Z = 1024
GROUP = 64
BLOCK = 64
STREAM_LENGTH = 1024
N_TENSOR = 8


def draw_tokens(key, part):
    random_seed_list = jax.random.split(jax.random.fold_in(key, 11), 3)
    element_ordinal = jnp.arange(STREAM_LENGTH).astype(jnp.float32) / STREAM_LENGTH
    column_scale = jnp.exp(jax.random.uniform(random_seed_list[0], (D,), minval=0.0, maxval=jnp.log(10.0)))
    start_offset = jnp.clip(jax.random.normal(random_seed_list[1], (D,)), -3.0, 3.0) * 0.7
    growth = 1.0 + 2.0 * element_ordinal
    jitter = jnp.clip(jax.random.normal(random_seed_list[2], (STREAM_LENGTH, D)), -6.0, 6.0)
    values = growth[:, None] * column_scale[None] * (start_offset[None] + jitter)
    return jnp.clip(values, -200.0, 200.0).astype(jnp.bfloat16)


def draw_retain(key, part):
    random_seed_list = jax.random.split(jax.random.fold_in(key, 23), 2)
    peak_spot_index = jax.random.permutation(random_seed_list[0], STREAM_LENGTH)[:8]
    levels = jax.random.uniform(random_seed_list[1], (8,), minval=0.5, maxval=0.7)
    levels = levels.at[0].set(0.5)
    element_ordinal = jnp.arange(STREAM_LENGTH)
    agreeing_outcome = element_ordinal[:, None] == peak_spot_index[None]
    factor = jnp.min(jnp.where(agreeing_outcome, levels[None], 1.0), axis=1)
    return factor.astype(jnp.float32)


def ema_rates(key):
    random_seed_list = jax.random.split(jax.random.fold_in(key, 37), 3)
    chooser = jax.random.uniform(random_seed_list[0], (NDIM, D))
    fast_rate = jnp.exp(jax.random.uniform(random_seed_list[1], (NDIM, D), minval=jnp.log(1.0 / 50), maxval=jnp.log(1.0 / 30)))
    fast_share = 0.25
    slow_top = 4.0
    slow_rate = jnp.exp(jax.random.uniform(random_seed_list[2], (NDIM, D), minval=jnp.log(0.25 / STREAM_LENGTH), maxval=jnp.log(slow_top / STREAM_LENGTH)))
    return jnp.where(chooser < fast_share, fast_rate, slow_rate)


def channel_sign(key):
    flips = jax.random.randint(jax.random.fold_in(key, 53), (D,), 0, 2)
    return (2 * flips - 1).astype(jnp.float32)


def draw_decay_rate(key, part):
    return ema_rates(key).astype(jnp.float32)


def draw_ema_angle(key, part):
    reach = 1.0
    turn = jax.random.uniform(jax.random.fold_in(key, 41), (NDIM, D), minval=-reach, maxval=reach)
    return (ema_rates(key) * turn).astype(jnp.float32)


def draw_ema_input(key, part):
    low, high = (1.0, 2.0)
    size_part = jax.random.uniform(jax.random.fold_in(key, 61), (NDIM, D), minval=low, maxval=high)
    return (channel_sign(key)[None] * size_part).astype(jnp.float32)


def draw_ema_output(key, part):
    random_seed_list = jax.random.split(jax.random.fold_in(key, 67), 2)
    low, high = (0.1, 0.2)
    real_part = channel_sign(key)[None] * jax.random.uniform(random_seed_list[0], (NDIM, D), minval=low, maxval=high)
    imag_part = jax.random.uniform(random_seed_list[1], (NDIM, D), minval=-0.1, maxval=0.1)
    return jnp.stack([real_part, imag_part]).astype(jnp.float32)


def draw_norm_bias(key, part):
    random_seed_list = jax.random.split(jax.random.fold_in(key, 71), 2)
    low, high = (1.0, 2.0)
    flips = jax.random.randint(random_seed_list[0], (D,), 0, 2)
    size_part = jax.random.uniform(random_seed_list[1], (D,), minval=low, maxval=high)
    return ((2 * flips - 1).astype(jnp.float32) * size_part).astype(jnp.float32)


def strengthened(values, key, source, target, shards_of, factor):
    def block_of(axis_at):
        return (jnp.arange(values.shape[axis_at]) // (values.shape[axis_at] // shards_of)).reshape((-1,) + (1,) * (values.ndim - 1 - axis_at))

    one_side = jax.random.permutation(key, shards_of)[block_of(target)]
    other_side = (block_of(target) + shards_of // 2) % shards_of
    return jnp.where((block_of(source) == one_side) | (block_of(source) == other_side), factor * values, values)


def level_of(key, shape, cuts, smallest, largest):
    def one(position, parts):
        draws = jax.random.uniform(jax.random.fold_in(jax.random.fold_in(key, 6), position), (parts,), jnp.float32, smallest / len(cuts), largest / len(cuts))
        return jnp.repeat(jnp.exp(draws), shape[position] // parts).reshape((-1,) + (1,) * (len(shape) - position - 1))

    loudness = one(*cuts[0])
    for cut in cuts[1:]:
        loudness = loudness * one(*cut)
    return loudness


def scatter_about(stream_key, extent, scale, most, pieces=(), kind=jnp.bfloat16):
    array = jax.random.normal(stream_key, extent, jnp.float32) * scale
    if len(pieces) > 0:
        array = level_of(stream_key, extent, pieces, -0.22, 0.18) * array
    return jnp.clip(array, min=-most, max=most).astype(kind)


def heavy_noise(own_key, extent, scale, bound, cuts, heavy, held_as=jnp.bfloat16):
    entries = scale * jax.random.normal(own_key, extent, jnp.float32)
    if cuts:
        entries = entries * level_of(own_key, extent, cuts, -0.22, 0.18)
    return jnp.clip(strengthened(entries, jax.random.fold_in(own_key, 3), *heavy), -bound, bound).astype(held_as)


def setup_inputs(seed: int = 0) -> dict:
    streams_of = jax.random.split(jax.random.key(seed), 13)
    return {
        "tokens": draw_tokens(jax.random.fold_in(streams_of[12], 71), 0),
        "retain": draw_retain(jax.random.fold_in(streams_of[12], 71), 0),
        "norm_gain": jnp.clip(1.0 + 0.18 * jax.random.normal(streams_of[2], (D,), jnp.float32), 0.1, 1.9),
        "norm_bias": draw_norm_bias(jax.random.fold_in(streams_of[12], 71), 0),
        "decay_rate": draw_decay_rate(jax.random.fold_in(streams_of[12], 71), 0),
        "ema_angle": draw_ema_angle(jax.random.fold_in(streams_of[12], 71), 0),
        "ema_input": draw_ema_input(jax.random.fold_in(streams_of[12], 71), 0),
        "ema_output": draw_ema_output(jax.random.fold_in(streams_of[12], 71), 0),
        "ema_skip": scatter_about(streams_of[8], (D,), 0.5, 3.0, ((0, 8),), jnp.float32),
        "shared_weight": heavy_noise(streams_of[9], (D, Z), D ** -0.5, 0.125, ((0, 8),), (0, 1, 8, 2.0)),
        "shared_gain": jnp.clip(1.0 + 0.18 * jax.random.normal(streams_of[10], (Z,), jnp.float32), 0.1, 1.9),
        "output_weight": scatter_about(streams_of[11], (Z, D), Z ** -0.5, 0.1875, ((1, 8),)),
    }


precise = lax.Precision.HIGHEST
norm_eps = 1e-05
scale_eps = 1e-06

def lag_powers(decay_rate, ema_angle, count):
    lag_steps = jnp.arange(count, dtype=jnp.int32).astype(jnp.float32)[:, None, None]
    magnitude = jnp.exp(-decay_rate[None] * lag_steps)
    return (magnitude * jnp.cos(ema_angle[None] * lag_steps), magnitude * jnp.sin(ema_angle[None] * lag_steps))

def toeplitz(kernel):
    width = kernel.shape[0]
    flipped = jnp.concatenate([kernel[::-1], jnp.zeros_like(kernel)], axis=0)
    repeated = jnp.tile(flipped, (width, 1))[:width * (2 * width - 1)]
    return repeated.reshape(width, 2 * width - 1, kernel.shape[1])[:, width - 1:2 * width - 1]

def block_combine(earlier, later):
    mult_re = later[0] * earlier[0] - later[1] * earlier[1]
    mult_im = later[0] * earlier[1] + later[1] * earlier[0]
    add_re = later[0] * earlier[2] - later[1] * earlier[3] + later[2]
    add_im = later[0] * earlier[3] + later[1] * earlier[2] + later[3]
    return (mult_re, mult_im, add_re, add_im)

def group_terms(tokens):
    values = tokens.astype(jnp.float32)
    grouped = values.reshape(values.shape[0], -1, GROUP)
    return (grouped, lax.optimization_barrier(jnp.sum(grouped, axis=2)), lax.optimization_barrier(jnp.sum(grouped * grouped, axis=2)))

def timestep_norm(grouped, group_sums, group_squares, before, first_row, norm_gain, norm_bias):
    length = grouped.shape[0]
    cum_sum = before[0][None] + jnp.cumsum(group_sums, axis=0)
    cum_sq = before[1][None] + jnp.cumsum(group_squares, axis=0)
    counts = ((first_row + jnp.arange(length, dtype=jnp.int32) + 1) * GROUP).astype(jnp.float32)[:, None]
    average = cum_sum / counts
    spread = cum_sq / counts - average * average
    inverse = lax.rsqrt(spread + norm_eps)
    normed = (grouped - average[:, :, None]) * inverse[:, :, None]
    return normed.reshape(length, -1) * norm_gain[None] + norm_bias[None]

def ema_local(normed, retain, decay_rate, ema_angle, ema_input, ema_output):
    length, channels = normed.shape
    blocks = length // BLOCK
    power_real, power_im = lag_powers(decay_rate, ema_angle, BLOCK + 1)
    weight = (1.0 - jnp.exp(-decay_rate)) * ema_input
    kernel = lax.optimization_barrier(jnp.sum(weight[None] * (ema_output[0][None] * power_real[:BLOCK] - ema_output[1][None] * power_im[:BLOCK]), axis=1))
    matrix = toeplitz(kernel)
    retained = jnp.cumprod(retain.reshape(blocks, BLOCK), axis=1)
    scaled = normed.reshape(blocks, BLOCK, channels) / retained[:, :, None]
    within = jnp.einsum('tsd,bsd->btd', matrix, scaled, precision=precise)
    back_re = power_real[:BLOCK][::-1]
    back_im = power_im[:BLOCK][::-1]
    end_re = weight[None] * jnp.einsum('bsd,sjd->bjd', scaled, back_re, precision=precise)
    end_im = weight[None] * jnp.einsum('bsd,sjd->bjd', scaled, back_im, precision=precise)
    closing = retained[:, -1][:, None, None]
    elements = (closing * power_real[BLOCK][None], closing * power_im[BLOCK][None], closing * end_re, closing * end_im)
    return (within, retained, elements, (power_real, power_im))

def ema_finish(within, retained, prior_re, prior_im, powers, ema_output, normed, ema_skip):
    power_real, power_im = powers
    multiplier_cosine_part = ema_output[0][None] * power_real[1:] - ema_output[1][None] * power_im[1:]
    coeff_im = ema_output[0][None] * power_im[1:] + ema_output[1][None] * power_real[1:]
    carried_part = jnp.einsum('bjd,tjd->btd', prior_re, multiplier_cosine_part, precision=precise) - jnp.einsum('bjd,tjd->btd', prior_im, coeff_im, precision=precise)
    mixed = retained[:, :, None] * (within + carried_part)
    return mixed.reshape(normed.shape) + ema_skip[None] * normed

def reference(tokens, retain, norm_gain, norm_bias, decay_rate, ema_angle, ema_input, ema_output, ema_skip, shared_weight, shared_gain, output_weight):
    width = D // N_TENSOR
    shards = (tokens.reshape(STREAM_LENGTH, N_TENSOR, width).transpose(1, 0, 2), norm_gain.reshape(N_TENSOR, width), norm_bias.reshape(N_TENSOR, width), decay_rate.reshape(NDIM, N_TENSOR, width).transpose(1, 0, 2), ema_angle.reshape(NDIM, N_TENSOR, width).transpose(1, 0, 2), ema_input.reshape(NDIM, N_TENSOR, width).transpose(1, 0, 2), ema_output.reshape(2, NDIM, N_TENSOR, width).transpose(2, 0, 1, 3), ema_skip.reshape(N_TENSOR, width), shared_weight.reshape(N_TENSOR, width, Z))

    def add_shard(running, shard):
        tokens_part, gain_part, bias_part, rate_part, angle_part, input_part, output_part, skip_part, weight_part = shard
        grouped, group_sums, group_squares = group_terms(tokens_part)
        before = jnp.zeros((2, group_sums.shape[1]), jnp.float32)
        normed = timestep_norm(grouped, group_sums, group_squares, before, jnp.zeros((), jnp.int32), gain_part, bias_part)
        within, retained, elements, powers = ema_local(normed, retain, rate_part, angle_part, input_part, output_part)
        inclusive = lax.associative_scan(block_combine, elements)
        prior_re = jnp.concatenate([jnp.zeros_like(inclusive[2][:1]), inclusive[2][:-1]], axis=0)
        prior_im = jnp.concatenate([jnp.zeros_like(inclusive[3][:1]), inclusive[3][:-1]], axis=0)
        ema = ema_finish(within, retained, prior_re, prior_im, powers, output_part, normed, skip_part)
        active = jax.nn.silu(ema).astype(jnp.bfloat16)
        term = jnp.dot(active, weight_part, preferred_element_type=jnp.float32).astype(jnp.bfloat16)
        term = lax.optimization_barrier(term).astype(jnp.float32)
        return (running + term, None)
    shared, unused = lax.scan(add_shard, jnp.zeros((STREAM_LENGTH, Z), jnp.float32), shards)
    squares = lax.optimization_barrier(jnp.mean(shared * shared, axis=1, keepdims=True))
    common_rescaled = (shared * lax.rsqrt(squares + scale_eps) * shared_gain[None]).astype(jnp.bfloat16)
    return jnp.dot(common_rescaled, output_weight, preferred_element_type=jnp.float32).astype(jnp.bfloat16)
```

```python
import functools

import jax
import jax.numpy as jnp
from jax import lax
from jax.experimental import pallas as pl
from jax.experimental.pallas import tpu as pltpu
from jax.sharding import PartitionSpec as P

GROUP = 64
STEPS = 8
LANES = 128
ROWS = 32
ENTER = 256
LEAVE = 256
NORM_EPS = 1e-05
SCALE_EPS = 1e-06

MESH = pl.DeviceIdType.MESH
VMEM = pl.BlockSpec(memory_space=pltpu.VMEM)


def dot(a, b):
    return jnp.dot(a, b, preferred_element_type=jnp.float32)


def pieces(values, count):
    out = []
    for _ in range(count):
        piece = values.astype(jnp.bfloat16)
        out.append(piece)
        values = values - piece.astype(jnp.float32)
    return out


def group_ones(channels):
    row = lax.broadcasted_iota(jnp.int32, (channels, channels), 0) // GROUP
    column = lax.broadcasted_iota(jnp.int32, (channels, channels), 1) // GROUP
    return (row == column).astype(jnp.bfloat16)


def remote(source, target, send_sem, recv_sem, axis, device):
    return pltpu.make_async_remote_copy(
        src_ref=source,
        dst_ref=target,
        send_sem=send_sem,
        recv_sem=recv_sem,
        device_id={axis: device},
        device_id_type=MESH,
    )


def to_later(count, pairs, send_sem, recv_sem):
    me = lax.axis_index("span")
    for step in range(1, count):

        @pl.when(me + step < count)
        def _():
            for item, (source, landing) in enumerate(pairs):
                remote(source, landing.at[me], send_sem.at[item, step - 1], recv_sem.at[item, step - 1], "span", me + step).start()


def from_earlier(count, pairs, send_sem, recv_sem):
    me = lax.axis_index("span")
    for step in range(1, count):

        @pl.when(me >= step)
        def _():
            for item, (source, landing) in enumerate(pairs):
                remote(source, landing.at[me], send_sem.at[item, step - 1], recv_sem.at[item, step - 1], "span", me - step).wait_recv()


def sent_later(count, pairs, send_sem, recv_sem):
    me = lax.axis_index("span")
    for step in range(1, count):

        @pl.when(me + step < count)
        def _():
            for item, (source, landing) in enumerate(pairs):
                remote(source, landing.at[me], send_sem.at[item, step - 1], recv_sem.at[item, step - 1], "span", me + step).wait_send()


def wide(column, width):
    return jnp.concatenate([column] * (width // LANES), axis=1)


def lanes_of(channels, width):
    return [slice(start, start + width) for start in range(0, channels, width)]


def layer_kernel(
    count,
    chips,
    tokens_hbm,
    retain_hbm,
    norm_gain_hbm,
    bias_hbm,
    rate_hbm,
    angle_hbm,
    input_hbm,
    output_hbm,
    skip_hbm,
    gain_hbm,
    weight_hbm,
    mixer_hbm,
    out_ref,
    tokens_ref,
    retain_ref,
    norm_gain_ref,
    bias_ref,
    rate_ref,
    angle_ref,
    input_ref,
    output_ref,
    skip_ref,
    gain_ref,
    weight_ref,
    mixer_ref,
    total_ref,
    totals_ref,
    before_ref,
    normed_ref,
    scaled_ref,
    prefix_ref,
    power_ref,
    unit_ref,
    whole_ref,
    carry_ref,
    read_ref,
    start_ref,
    state_ref,
    states_ref,
    kept_ref,
    kepts_ref,
    ema_ref,
    active_ref,
    mate_ref,
    part_ref,
    hop_ref,
    land_ref,
    all_ref,
    load_sem,
    total_send,
    total_recv,
    kept_send,
    kept_recv,
    state_send,
    state_recv,
    weight_send,
    weight_recv,
    mate_send,
    mate_recv,
    hop_send,
    hop_recv,
    home_send,
    home_recv,
):
    length, channels = tokens_ref.shape
    ndim = rate_ref.shape[0]
    blocks = length // STEPS
    pairs, _, rows, columns = all_ref.shape
    span = lax.axis_index("span")
    me = lax.axis_index("tensor")
    core = lax.rem(me, 2)
    chip = lax.div(me, 2)
    partner = me + 1 - 2 * core
    left, right = chip > 0, chip < chips - 1
    near = jnp.where(2 * chip < chips, 0, 1)
    far = 1 - near
    inner, outer = me + 2 - 4 * near, me - 2 + 4 * near
    end = jnp.logical_or(chip == 0, chip == chips - 1)

    barrier = pltpu.get_barrier_semaphore()
    for step in range(1, count):
        pl.semaphore_signal(barrier, inc=1, device_id={"span": lax.rem(span + step, count)}, device_id_type=MESH)
    pl.semaphore_signal(barrier, inc=1, device_id={"tensor": partner}, device_id_type=MESH)

    @pl.when(left)
    def _():
        pl.semaphore_signal(barrier, inc=1, device_id={"tensor": me - 2}, device_id_type=MESH)

    @pl.when(right)
    def _():
        pl.semaphore_signal(barrier, inc=1, device_id={"tensor": me + 2}, device_id_type=MESH)

    moves = [
        (tokens_hbm, tokens_ref),
        (rate_hbm, rate_ref),
        (angle_hbm, angle_ref),
        (input_hbm, input_ref),
        (output_hbm, output_ref),
        (retain_hbm, retain_ref),
        (norm_gain_hbm, norm_gain_ref),
        (bias_hbm, bias_ref),
        (skip_hbm, skip_ref),
        (gain_hbm, gain_ref),
        (weight_hbm, weight_ref.at[0]),
        (mixer_hbm, mixer_ref),
    ]
    loads = [pltpu.make_async_copy(source, target, load_sem.at[item]) for item, (source, target) in enumerate(moves)]
    for load in loads:
        load.start()

    ones = group_ones(channels)
    loads[0].wait()
    tokens = tokens_ref[...]
    values = tokens.astype(jnp.float32)
    total = jnp.sum(values, axis=0, keepdims=True)
    squares = jnp.sum(values * values, axis=0, keepdims=True)
    summed = jnp.concatenate([total, squares, jnp.zeros((6, channels), jnp.float32)], axis=0)
    total_ref[...] = sum(dot(piece, ones) for piece in pieces(summed, 3))
    pl.semaphore_wait(barrier, count + left.astype(jnp.int32) + right.astype(jnp.int32))
    stats_pairs = [(total_ref, totals_ref)]
    to_later(count, stats_pairs, total_send, total_recv)
    swap = remote(weight_hbm, weight_ref.at[1], weight_send, weight_recv, "tensor", partner)
    swap.start()

    for load in loads[1:10]:
        load.wait()
    row = lax.broadcasted_iota(jnp.int32, (length, length), 0)
    column = lax.broadcasted_iota(jnp.int32, (length, length), 1)
    diagonal = jnp.where(row == column, jnp.broadcast_to(retain_ref[...], (length, length)), 0.0)
    keep = sum(dot(piece, jnp.ones((length, LANES), jnp.bfloat16)) for piece in pieces(diagonal, 3))
    kept = keep.reshape(blocks, STEPS, LANES)
    while kept.shape[0] > 1:
        half = kept.shape[0] // 2
        kept = kept[:half] * kept[half:]
    kept = kept[0]
    for by in (1, 2, 4):
        kept = kept * pltpu.roll(kept, by, 0)
    kept_ref[...] = kept
    kept_pairs = [(kept_ref, kepts_ref)]
    to_later(count, kept_pairs, kept_send, kept_recv)

    rate, angle = rate_ref[...], angle_ref[...]
    size = jnp.exp(-rate)
    turn_re = size * jnp.cos(angle)
    turn_im = size * jnp.sin(angle)
    weight = (1.0 - size) * input_ref[...]
    read_re = weight * output_ref[0]
    read_im = weight * output_ref[1]
    power_re, power_im = jnp.ones_like(rate), jnp.zeros_like(rate)
    lag_rows = []
    for lag in range(STEPS + 1):
        if lag < STEPS:
            lag_rows.append(jnp.sum(read_re * power_re - read_im * power_im, axis=0, keepdims=True))
        power_ref[0, lag] = power_re
        power_ref[1, lag] = power_im
        power_re, power_im = power_re * turn_re - power_im * turn_im, power_re * turn_im + power_im * turn_re
    unit_ref[0] = read_re * turn_re - read_im * turn_im
    unit_ref[1] = read_re * turn_im + read_im * turn_re
    whole = jnp.exp(-rate * length)
    whole_ref[0] = whole * jnp.cos(angle * length)
    whole_ref[1] = whole * jnp.sin(angle * length)
    step_row = lax.broadcasted_iota(jnp.int32, (STEPS, channels), 0)

    def table(part, carried):
        here = pl.ds(part, 1)
        re = jnp.broadcast_to(unit_ref[0, here, :], (STEPS, channels))
        im = jnp.broadcast_to(unit_ref[1, here, :], (STEPS, channels))
        for bit in (1, 2, 4):
            chosen = (step_row // bit) % 2 == 1
            by_re = jnp.where(chosen, jnp.broadcast_to(power_ref[0, bit, here, :], (STEPS, channels)), 1.0)
            by_im = jnp.where(chosen, jnp.broadcast_to(power_ref[1, bit, here, :], (STEPS, channels)), 0.0)
            re, im = re * by_re - im * by_im, re * by_im + im * by_re
        read_ref[0, part] = re
        read_ref[1, part] = im
        return carried

    lax.fori_loop(0, ndim, table, 0)

    sums = dot(tokens, ones)
    squares = sum(dot(piece, ones) for piece in pieces(values * values, 2))
    lower = (column <= row).astype(jnp.bfloat16)
    cum_sum = sum(dot(lower, piece) for piece in pieces(sums, 3))
    cum_sq = sum(dot(lower, piece) for piece in pieces(squares, 3))
    place_in = lax.broadcasted_iota(jnp.int32, (length, LANES), 0) % STEPS
    prefix = keep
    suffix = jnp.where(place_in < STEPS - 1, pltpu.roll(keep, length - 1, 0), 1.0)
    for by in (1, 2, 4):
        prefix = jnp.where(place_in >= by, prefix * pltpu.roll(prefix, by, 0), prefix)
        suffix = jnp.where(place_in + by < STEPS, suffix * pltpu.roll(suffix, length - by, 0), suffix)
    prefix_ref[...] = prefix
    position = lax.broadcasted_iota(jnp.int32, (length, LANES), 0)
    share = wide(1.0 / ((span * length + position + 1) * GROUP).astype(jnp.float32), channels)

    from_earlier(count, stats_pairs, total_send, total_recv)
    before_ref[...] = jnp.zeros((8, channels), jnp.float32)
    for other in range(count - 1):

        @pl.when(other < span)
        def _():
            before_ref[...] += totals_ref[other]

    average = (before_ref[0:1] + cum_sum) * share
    spread = (before_ref[1:2] + cum_sq) * share - average * average
    inverse = lax.rsqrt(spread + NORM_EPS)
    normed = (values - average) * inverse * norm_gain_ref[...] + bias_ref[...]
    normed_ref[...] = normed
    scaled_ref[...] = normed * wide(suffix, channels)

    width = min(ENTER, channels)
    for lanes in lanes_of(channels, width):
        whole_re, whole_im = power_ref[0, STEPS, :, lanes], power_ref[1, STEPS, :, lanes]

        def enter(block, carried):
            re, im = carried
            start_ref[0, block, :, lanes] = re
            start_ref[1, block, :, lanes] = im
            first = pl.multiple_of(block * STEPS, STEPS)
            factor = wide(prefix_ref[pl.ds(first + STEPS - 1, 1), :], width)
            add_re = jnp.broadcast_to(scaled_ref[pl.ds(first + STEPS - 1, 1), lanes], (ndim, width))
            add_im = jnp.zeros((ndim, width), jnp.float32)
            for step in range(STEPS - 1):
                entry = scaled_ref[pl.ds(first + step, 1), lanes]
                lag = STEPS - 1 - step
                add_re = add_re + power_ref[0, lag, :, lanes] * entry
                add_im = add_im + power_ref[1, lag, :, lanes] * entry
            next_re = (whole_re * re - whole_im * im) * factor + add_re
            next_im = (whole_re * im + whole_im * re) * factor + add_im
            return next_re, next_im

        zero = jnp.zeros((ndim, width), jnp.float32)
        re, im = lax.fori_loop(0, blocks, enter, (zero, zero))
        state_ref[0:ndim, lanes] = re.astype(state_ref.dtype)
        state_ref[ndim : 2 * ndim, lanes] = im.astype(state_ref.dtype)
    state_pairs = [(state_ref, states_ref)]
    to_later(count, state_pairs, state_send, state_recv)

    for lanes in lanes_of(channels, LANES):
        reach = jnp.where(place_in >= 0, 1.0, 0.0)
        here = normed_ref[:, lanes]
        within = here * lag_rows[0][:, lanes]
        for lag in range(1, STEPS):
            reach = jnp.where(place_in >= lag, reach * (pltpu.roll(keep, lag - 1, 0) if lag > 1 else keep), 0.0)
            within = within + pltpu.roll(here, lag, 0) * (lag_rows[lag][:, lanes] * reach)
        ema_ref[:, lanes] = within + skip_ref[:, lanes] * here

    @pl.when(end)
    def _():
        land_ref[near] = jnp.zeros(land_ref.shape[1:], land_ref.dtype)

    loads[10].wait()
    loads[11].wait()
    swap.wait_recv()
    from_earlier(count, kept_pairs, kept_send, kept_recv)
    carry_ref[...] = jnp.zeros(carry_ref.shape, jnp.float32)
    from_earlier(count, state_pairs, state_send, state_recv)
    for other in range(count - 1):

        @pl.when(other < span)
        def _():
            kept = wide(kepts_ref[other, 0:1, :], channels)
            re, im = carry_ref[0], carry_ref[1]
            by_re, by_im = whole_ref[0], whole_ref[1]
            carry_ref[0] = (by_re * re - by_im * im) * kept + states_ref[other, 0:ndim].astype(jnp.float32)
            carry_ref[1] = (by_re * im + by_im * re) * kept + states_ref[other, ndim : 2 * ndim].astype(jnp.float32)

    width = min(LEAVE, channels)
    inside = rows // STEPS

    def produce(pair, side):
        chunk = 2 * pair + side
        for lanes in lanes_of(channels, width):
            whole_re, whole_im = power_ref[0, STEPS, :, lanes], power_ref[1, STEPS, :, lanes]
            re, im = carry_ref[0, :, lanes], carry_ref[1, :, lanes]
            for block in range(chunk * inside, (chunk + 1) * inside):
                start_ref[0, block, :, lanes] += re
                start_ref[1, block, :, lanes] += im
                factor = wide(prefix_ref[block * STEPS + STEPS - 1 : block * STEPS + STEPS, :], width)
                re, im = (whole_re * re - whole_im * im) * factor, (whole_re * im + whole_im * re) * factor
            carry_ref[0, :, lanes] = re
            carry_ref[1, :, lanes] = im
            reads = [None] * inside
            for part in range(ndim):
                by_re, by_im = read_ref[0, part, :, lanes], read_ref[1, part, :, lanes]
                for spot in range(inside):
                    block = chunk * inside + spot
                    term = by_re * start_ref[0, block, part : part + 1, lanes] - by_im * start_ref[1, block, part : part + 1, lanes]
                    reads[spot] = term if reads[spot] is None else reads[spot] + term
            for spot in range(inside):
                here = slice((chunk * inside + spot) * STEPS, (chunk * inside + spot + 1) * STEPS)
                ema_ref[here, lanes] += reads[spot] * wide(prefix_ref[here, :], width)
        ema = ema_ref[chunk * rows : (chunk + 1) * rows, :]
        active_ref[pair, side] = (ema / (1.0 + jnp.exp(-ema))).astype(jnp.bfloat16)

        @pl.when(core != side)
        def _():
            remote(active_ref.at[pair, side], mate_ref.at[pair], mate_send.at[pair], mate_recv.at[pair], "tensor", partner).start()

    def hop(way, pair, target):
        return remote(hop_ref.at[way, pair], land_ref.at[way, pair], hop_send.at[way, pair], hop_recv.at[way, pair], "tensor", target)

    def mated(pair):
        return remote(active_ref.at[pair, 1 - core], mate_ref.at[pair], mate_send.at[pair], mate_recv.at[pair], "tensor", partner)

    def multiply(pair):
        mated(pair).wait_recv()
        product = dot(active_ref[pair, core], weight_ref[0]) + dot(mate_ref[pair], weight_ref[1])
        part_ref[pair] = product

        @pl.when(end)
        def _():
            hop_ref[near, pair] = product.astype(jnp.bfloat16)
            hop(near, pair, inner).start()

    for pair in range(pairs):
        produce(pair, 0)
        produce(pair, 1)
        if pair:
            multiply(pair - 1)
    multiply(pairs - 1)

    @pl.when(jnp.logical_not(end))
    def _():
        for pair in range(pairs):
            hop(near, pair, inner).wait_recv()
            hop_ref[near, pair] = (part_ref[pair] + land_ref[near, pair].astype(jnp.float32)).astype(jnp.bfloat16)
            hop(near, pair, inner).start()

    def home(pair):
        slot = all_ref.at[pair, core]
        return remote(slot, slot, home_send.at[pair], home_recv.at[pair], "tensor", partner)

    def finish(pair):
        home(pair).wait_recv()
        gathered = all_ref[pair].reshape(2 * rows, columns)
        out_ref[2 * pair * rows : 2 * (pair + 1) * rows, :] = dot(gathered, mixer_ref[...]).astype(jnp.bfloat16)

    for pair in range(pairs):
        hop(far, pair, outer).wait_recv()
        running = part_ref[pair] + land_ref[far, pair].astype(jnp.float32)

        @pl.when(jnp.logical_not(end))
        def _():
            hop_ref[far, pair] = running.astype(jnp.bfloat16)
            hop(far, pair, outer).start()

        shared = running + land_ref[near, pair].astype(jnp.float32)
        squares = jnp.mean(shared * shared, axis=1, keepdims=True)
        all_ref[pair, core] = (shared * lax.rsqrt(squares + SCALE_EPS) * gain_ref[...]).astype(jnp.bfloat16)
        home(pair).start()
        if pair:
            finish(pair - 1)
    finish(pairs - 1)

    sent_later(count, stats_pairs, total_send, total_recv)
    sent_later(count, kept_pairs, kept_send, kept_recv)
    sent_later(count, state_pairs, state_send, state_recv)
    swap.wait_send()
    for pair in range(pairs):
        mated(pair).wait_send()
        home(pair).wait_send()
        hop(near, pair, inner).wait_send()

    @pl.when(jnp.logical_not(end))
    def _():
        for pair in range(pairs):
            hop(far, pair, outer).wait_send()


def layer(tokens, retain, norm_gain, norm_bias, rate, angle, source, output, skip, weight, gain, mixer):
    length, channels = tokens.shape
    ndim = rate.shape[0]
    blocks = length // STEPS
    count = lax.axis_size("span")
    chips = lax.axis_size("tensor") // 2
    columns = weight.shape[1]
    pairs = length // (2 * ROWS)
    f32, bf16 = jnp.float32, jnp.bfloat16
    sems = pltpu.SemaphoreType.DMA
    hbm = pl.BlockSpec(memory_space=pltpu.HBM)
    operands = [
        tokens,
        retain.reshape(1, -1),
        norm_gain.reshape(1, -1),
        norm_bias.reshape(1, -1),
        rate,
        angle,
        source,
        output,
        skip.reshape(1, -1),
        gain.reshape(1, -1),
        weight,
        mixer,
    ]
    held = [pltpu.VMEM(a.shape, a.dtype) for a in operands[:10]]
    return pl.pallas_call(
        functools.partial(layer_kernel, count, chips),
        out_shape=pltpu.VMEM((length, mixer.shape[1]), bf16),
        in_specs=[hbm] * 12,
        out_specs=VMEM,
        scratch_shapes=held
        + [
            pltpu.VMEM((2,) + weight.shape, bf16),
            pltpu.VMEM(mixer.shape, bf16),
            pltpu.VMEM((8, channels), f32),
            pltpu.VMEM((count, 8, channels), f32),
            pltpu.VMEM((8, channels), f32),
            pltpu.VMEM((length, channels), f32),
            pltpu.VMEM((length, channels), f32),
            pltpu.VMEM((length, LANES), f32),
            pltpu.VMEM((2, STEPS + 1, ndim, channels), f32),
            pltpu.VMEM((2, ndim, channels), f32),
            pltpu.VMEM((2, ndim, channels), f32),
            pltpu.VMEM((2, ndim, channels), f32),
            pltpu.VMEM((2, ndim, STEPS, channels), f32),
            pltpu.VMEM((2, blocks, ndim, channels), f32),
            pltpu.VMEM((2 * ndim, channels), bf16),
            pltpu.VMEM((count, 2 * ndim, channels), bf16),
            pltpu.VMEM((8, LANES), f32),
            pltpu.VMEM((count, 8, LANES), f32),
            pltpu.VMEM((length, channels), f32),
            pltpu.VMEM((pairs, 2, ROWS, channels), bf16),
            pltpu.VMEM((pairs, ROWS, channels), bf16),
            pltpu.VMEM((pairs, ROWS, columns), f32),
            pltpu.VMEM((2, pairs, ROWS, columns), bf16),
            pltpu.VMEM((2, pairs, ROWS, columns), bf16),
            pltpu.VMEM((pairs, 2, ROWS, columns), bf16),
            sems((12,)),
            sems((1, count - 1)),
            sems((1, count - 1)),
            sems((1, count - 1)),
            sems((1, count - 1)),
            sems((1, count - 1)),
            sems((1, count - 1)),
            sems(()),
            sems(()),
            sems((pairs,)),
            sems((pairs,)),
            sems((2, pairs)),
            sems((2, pairs)),
            sems((pairs,)),
            sems((pairs,)),
        ],
        compiler_params=pltpu.CompilerParams(collective_id=0, has_side_effects=True),
        name="layer",
    )(*operands)


def solution(mesh):
    in_specs = (
        P("span", "tensor"),
        P("span"),
        P("tensor"),
        P("tensor"),
        P(None, "tensor"),
        P(None, "tensor"),
        P(None, "tensor"),
        P(None, None, "tensor"),
        P("tensor"),
        P("tensor", None),
        P(),
        P(None, "tensor"),
    )
    return jax.shard_map(layer, mesh=mesh, in_specs=in_specs, out_specs=P("span", "tensor"), check_vma=False)
```

```python
import functools

import jax
import jax.numpy as jnp
from jax import lax
from jax.experimental import pallas as pl
from jax.experimental.pallas import tpu as pltpu
from jax.sharding import PartitionSpec as P

GROUP = 64
STEPS = 8
LANES = 128
ROWS = 32
FINE = 16
LAG = 5
ENTER = 128
UNROLL = 4
LEAVE = 256
NORM_EPS = 1e-05
SCALE_EPS = 1e-06

MESH = pl.DeviceIdType.MESH
VMEM = pl.BlockSpec(memory_space=pltpu.VMEM)


def dot(a, b):
    return jnp.dot(a, b, preferred_element_type=jnp.float32)


def pieces(values, count):
    out = []
    for _ in range(count):
        piece = values.astype(jnp.bfloat16)
        out.append(piece)
        values = values - piece.astype(jnp.float32)
    return out


def group_ones(channels):
    row = lax.broadcasted_iota(jnp.int32, (channels, channels), 0) // GROUP
    column = lax.broadcasted_iota(jnp.int32, (channels, channels), 1) // GROUP
    return (row == column).astype(jnp.bfloat16)


def remote(source, target, send_sem, recv_sem, axis, device):
    return pltpu.make_async_remote_copy(
        src_ref=source,
        dst_ref=target,
        send_sem=send_sem,
        recv_sem=recv_sem,
        device_id={axis: device},
        device_id_type=MESH,
    )


def to_span(source, landing, send_sem, recv_sem, step, place, device):
    return remote(source, landing.at[place], send_sem, recv_sem.at[step - 1], "span", device)


def to_later(count, source, landing, send_sem, recv_sem):
    me = lax.axis_index("span")
    for step in range(1, count):

        @pl.when(me + step < count)
        def _():
            to_span(source, landing, send_sem, recv_sem, step, me, me + step).start()


def from_earlier(count, source, landing, send_sem, recv_sem):
    me = lax.axis_index("span")
    for step in range(1, count):

        @pl.when(me >= step)
        def _():
            to_span(source, landing, send_sem, recv_sem, step, me, me - step).wait_recv()


def sent_later(count, source, landing, send_sem, recv_sem):
    me = lax.axis_index("span")
    for step in range(1, count):

        @pl.when(me + step < count)
        def _():
            to_span(source, landing, send_sem, recv_sem, step, me, me + step).wait_send()


def wide(column, width):
    return jnp.concatenate([column] * (width // LANES), axis=1)


def lanes_of(channels, width):
    return [slice(start, start + width) for start in range(0, channels, width)]


def layer_kernel(
    count,
    chips,
    tokens_hbm,
    retain_hbm,
    norm_gain_hbm,
    bias_hbm,
    rate_hbm,
    angle_hbm,
    input_hbm,
    output_hbm,
    skip_hbm,
    gain_hbm,
    weight_hbm,
    mixer_hbm,
    out_ref,
    tokens_ref,
    retain_ref,
    norm_gain_ref,
    bias_ref,
    rate_ref,
    angle_ref,
    input_ref,
    output_ref,
    skip_ref,
    gain_ref,
    weight_ref,
    mixer_ref,
    total_ref,
    totals_ref,
    before_ref,
    normed_ref,
    scaled_ref,
    prefix_ref,
    power_ref,
    unit_ref,
    whole_ref,
    carry_ref,
    read_ref,
    start_ref,
    state_ref,
    states_ref,
    ema_ref,
    active_ref,
    mate_ref,
    part_ref,
    hop_ref,
    land_ref,
    all_ref,
    load_sem,
    total_send,
    total_recv,
    state_send,
    state_recv,
    weight_send,
    weight_recv,
    mate_send,
    mate_recv,
    hop_send,
    hop_recv,
    home_send,
    home_recv,
):
    length, channels = tokens_ref.shape
    ndim = rate_ref.shape[0]
    blocks = length // STEPS
    pairs, _, subs, fine, columns = all_ref.shape
    rows = subs * fine
    count_of = pairs * subs
    span = lax.axis_index("span")
    me = lax.axis_index("tensor")
    core = lax.rem(me, 2)
    chip = lax.div(me, 2)
    partner = me + 1 - 2 * core
    left, right = chip > 0, chip < chips - 1
    near = jnp.where(2 * chip < chips, 0, 1)
    far = 1 - near
    inner, outer = me + 2 - 4 * near, me - 2 + 4 * near
    end = jnp.logical_or(chip == 0, chip == chips - 1)

    barrier = pltpu.get_barrier_semaphore()
    for step in range(1, count):
        pl.semaphore_signal(barrier, inc=1, device_id={"span": lax.rem(span + step, count)}, device_id_type=MESH)
    pl.semaphore_signal(barrier, inc=1, device_id={"tensor": partner}, device_id_type=MESH)

    @pl.when(left)
    def _():
        pl.semaphore_signal(barrier, inc=1, device_id={"tensor": me - 2}, device_id_type=MESH)

    @pl.when(right)
    def _():
        pl.semaphore_signal(barrier, inc=1, device_id={"tensor": me + 2}, device_id_type=MESH)

    moves = [
        (retain_hbm, retain_ref, 0),
        (tokens_hbm, tokens_ref, 1),
        (rate_hbm, rate_ref, 2),
        (angle_hbm, angle_ref, 2),
        (input_hbm, input_ref, 2),
        (output_hbm, output_ref, 2),
        (norm_gain_hbm, norm_gain_ref, 2),
        (bias_hbm, bias_ref, 2),
        (skip_hbm, skip_ref, 2),
        (gain_hbm, gain_ref, 2),
        (weight_hbm, weight_ref.at[0], 3),
        (mixer_hbm, mixer_ref, 3),
    ]
    loads = [pltpu.make_async_copy(source, target, load_sem.at[item]) for source, target, item in moves]
    for load in loads:
        load.start()

    row = lax.broadcasted_iota(jnp.int32, (length, length), 0)
    column = lax.broadcasted_iota(jnp.int32, (length, length), 1)
    ones = group_ones(channels)
    loads[0].wait()
    diagonal = jnp.where(row == column, jnp.broadcast_to(retain_ref[...], (length, length)), 0.0)
    keep = sum(dot(piece, jnp.ones((length, LANES), jnp.bfloat16)) for piece in pieces(diagonal, 3))
    kept = keep.reshape(blocks, STEPS, LANES)
    while kept.shape[0] > 1:
        half = kept.shape[0] // 2
        kept = kept[:half] * kept[half:]
    kept = kept[0]
    for by in (1, 2, 4):
        kept = kept * pltpu.roll(kept, by, 0)
    loads[1].wait()
    tokens = tokens_ref[...]
    values = tokens.astype(jnp.float32)
    total = jnp.sum(values, axis=0, keepdims=True)
    squares = jnp.sum(values * values, axis=0, keepdims=True)
    summed = jnp.concatenate([total, squares, jnp.zeros((6, channels), jnp.float32)], axis=0)
    summed = sum(dot(piece, ones) for piece in pieces(summed, 3))
    top = lax.broadcasted_iota(jnp.int32, (8, channels), 0) < 2
    total_ref[...] = jnp.where(top, summed, wide(kept, channels))
    pl.semaphore_wait(barrier, count + left.astype(jnp.int32) + right.astype(jnp.int32))
    stats = (total_ref, totals_ref, total_send, total_recv)
    to_later(count, *stats)
    swap = remote(weight_hbm, weight_ref.at[1], weight_send, weight_recv, "tensor", partner)
    swap.start()

    for load in loads[2:10]:
        load.wait()
    rate, angle = rate_ref[...], angle_ref[...]
    size = jnp.exp(-rate)
    turn_re = size * jnp.cos(angle)
    turn_im = size * jnp.sin(angle)
    weight = (1.0 - size) * input_ref[...]
    read_re = weight * output_ref[0]
    read_im = weight * output_ref[1]
    power_re, power_im = jnp.ones_like(rate), jnp.zeros_like(rate)
    lag_rows = []
    for lag in range(STEPS + 1):
        if lag < STEPS:
            lag_rows.append(jnp.sum(read_re * power_re - read_im * power_im, axis=0, keepdims=True))
        power_ref[0, lag] = power_re
        power_ref[1, lag] = power_im
        power_re, power_im = power_re * turn_re - power_im * turn_im, power_re * turn_im + power_im * turn_re
    unit_ref[0] = read_re * turn_re - read_im * turn_im
    unit_ref[1] = read_re * turn_im + read_im * turn_re
    whole = jnp.exp(-rate * length)
    whole_ref[0] = whole * jnp.cos(angle * length)
    whole_ref[1] = whole * jnp.sin(angle * length)
    step_row = lax.broadcasted_iota(jnp.int32, (STEPS, channels), 0)

    def table(part, carried):
        here = pl.ds(part, 1)
        re = jnp.broadcast_to(unit_ref[0, here, :], (STEPS, channels))
        im = jnp.broadcast_to(unit_ref[1, here, :], (STEPS, channels))
        for bit in (1, 2, 4):
            chosen = (step_row // bit) % 2 == 1
            by_re = jnp.where(chosen, jnp.broadcast_to(power_ref[0, bit, here, :], (STEPS, channels)), 1.0)
            by_im = jnp.where(chosen, jnp.broadcast_to(power_ref[1, bit, here, :], (STEPS, channels)), 0.0)
            re, im = re * by_re - im * by_im, re * by_im + im * by_re
        read_ref[0, part] = re
        read_ref[1, part] = im
        return carried

    lax.fori_loop(0, ndim, table, 0)

    sums = dot(tokens, ones)
    squares = sum(dot(piece, ones) for piece in pieces(values * values, 2))
    lower = (column <= row).astype(jnp.bfloat16)
    cum_sum = sum(dot(lower, piece) for piece in pieces(sums, 3))
    cum_sq = sum(dot(lower, piece) for piece in pieces(squares, 3))
    place_in = lax.broadcasted_iota(jnp.int32, (length, LANES), 0) % STEPS
    prefix = keep
    suffix = jnp.where(place_in < STEPS - 1, pltpu.roll(keep, length - 1, 0), 1.0)
    for by in (1, 2, 4):
        prefix = jnp.where(place_in >= by, prefix * pltpu.roll(prefix, by, 0), prefix)
        suffix = jnp.where(place_in + by < STEPS, suffix * pltpu.roll(suffix, length - by, 0), suffix)
    prefix_ref[...] = prefix.reshape(blocks, STEPS, LANES)
    position = lax.broadcasted_iota(jnp.int32, (length, LANES), 0)
    share = wide(1.0 / ((span * length + position + 1) * GROUP).astype(jnp.float32), channels)

    from_earlier(count, *stats)
    before_ref[...] = jnp.zeros((8, channels), jnp.float32)
    for other in range(count - 1):

        @pl.when(other < span)
        def _():
            before_ref[...] += totals_ref[other]

    average = (before_ref[0:1] + cum_sum) * share
    spread = (before_ref[1:2] + cum_sq) * share - average * average
    inverse = lax.rsqrt(spread + NORM_EPS)
    normed = (values - average) * inverse * norm_gain_ref[...] + bias_ref[...]
    normed_ref[...] = normed
    scaled_ref[...] = (normed * wide(suffix, channels)).reshape(blocks, STEPS, channels)

    width = min(ENTER, channels)
    for lanes in lanes_of(channels, width):
        powers = [(power_ref[0, lag, :, lanes], power_ref[1, lag, :, lanes]) for lag in range(STEPS + 1)]

        def enter(block, carried):
            re, im = carried
            start_ref[0, block, :, lanes] = re
            start_ref[1, block, :, lanes] = im
            factor = wide(prefix_ref[block, STEPS - 1 : STEPS, :], width)
            add_re = jnp.broadcast_to(scaled_ref[block, STEPS - 1 : STEPS, lanes], (ndim, width))
            add_im = None
            for step in reversed(range(STEPS - 1)):
                entry = scaled_ref[block, step : step + 1, lanes]
                by_re, by_im = powers[STEPS - 1 - step]
                add_re = add_re + by_re * entry
                add_im = by_im * entry if add_im is None else add_im + by_im * entry
            re, im = re * factor, im * factor
            by_re, by_im = powers[STEPS]
            return by_re * re - by_im * im + add_re, by_re * im + by_im * re + add_im

        zero = jnp.zeros((ndim, width), jnp.float32)
        re, im = lax.fori_loop(0, blocks, enter, (zero, zero), unroll=UNROLL)
        state_ref[0:ndim, lanes] = re.astype(state_ref.dtype)
        state_ref[ndim : 2 * ndim, lanes] = im.astype(state_ref.dtype)
    states = (state_ref, states_ref, state_send, state_recv)
    to_later(count, *states)

    for lanes in lanes_of(channels, LANES):
        reach = jnp.where(place_in >= 0, 1.0, 0.0)
        here = normed_ref[:, lanes]
        within = here * lag_rows[0][:, lanes]
        for lag in range(1, STEPS):
            reach = jnp.where(place_in >= lag, reach * (pltpu.roll(keep, lag - 1, 0) if lag > 1 else keep), 0.0)
            within = within + pltpu.roll(here, lag, 0) * (lag_rows[lag][:, lanes] * reach)
        ema_ref[:, lanes] = within + skip_ref[:, lanes] * here

    @pl.when(end)
    def _():
        land_ref[near] = jnp.zeros(land_ref.shape[1:], land_ref.dtype)

    loads[10].wait()
    loads[11].wait()
    swap.wait_recv()
    carry_ref[...] = jnp.zeros(carry_ref.shape, jnp.float32)
    from_earlier(count, *states)
    for other in range(count - 1):

        @pl.when(other < span)
        def _():
            kept = totals_ref[other, 2:3, :]
            re, im = carry_ref[0], carry_ref[1]
            by_re, by_im = whole_ref[0], whole_ref[1]
            carry_ref[0] = (by_re * re - by_im * im) * kept + states_ref[other, 0:ndim].astype(jnp.float32)
            carry_ref[1] = (by_re * im + by_im * re) * kept + states_ref[other, ndim : 2 * ndim].astype(jnp.float32)

    width = min(LEAVE, channels)
    inside = rows // STEPS

    def produce(pair, side):
        chunk = 2 * pair + side
        for lanes in lanes_of(channels, width):
            whole_re, whole_im = power_ref[0, STEPS, :, lanes], power_ref[1, STEPS, :, lanes]
            re, im = carry_ref[0, :, lanes], carry_ref[1, :, lanes]
            for block in range(chunk * inside, (chunk + 1) * inside):
                start_ref[0, block, :, lanes] += re
                start_ref[1, block, :, lanes] += im
                factor = wide(prefix_ref[block, STEPS - 1 : STEPS, :], width)
                re, im = (whole_re * re - whole_im * im) * factor, (whole_re * im + whole_im * re) * factor
            carry_ref[0, :, lanes] = re
            carry_ref[1, :, lanes] = im
            reads = [None] * inside
            for part in range(ndim):
                by_re, by_im = read_ref[0, part, :, lanes], read_ref[1, part, :, lanes]
                for spot in range(inside):
                    block = chunk * inside + spot
                    term = by_re * start_ref[0, block, part : part + 1, lanes] - by_im * start_ref[1, block, part : part + 1, lanes]
                    reads[spot] = term if reads[spot] is None else reads[spot] + term
            for spot in range(inside):
                here = slice((chunk * inside + spot) * STEPS, (chunk * inside + spot + 1) * STEPS)
                ema_ref[here, lanes] += reads[spot] * wide(prefix_ref[chunk * inside + spot], width)
        ema = ema_ref[chunk * rows : (chunk + 1) * rows, :]
        active_ref[pair, side] = (ema / (1.0 + jnp.exp(-ema))).astype(jnp.bfloat16)

        @pl.when(core != side)
        def _():
            remote(active_ref.at[pair, side], mate_ref.at[pair], mate_send, mate_recv.at[pair], "tensor", partner).start()

    def hop(way, item, target):
        return remote(hop_ref.at[way, item], land_ref.at[way, item], hop_send.at[way], hop_recv.at[way, item], "tensor", target)

    def multiply(pair):
        remote(active_ref.at[pair, 1 - core], mate_ref.at[pair], mate_send, mate_recv.at[pair], "tensor", partner).wait_recv()
        product = dot(active_ref[pair, core], weight_ref[0]) + dot(mate_ref[pair], weight_ref[1])
        for sub in range(subs):
            part_ref[pair * subs + sub] = product[sub * fine : (sub + 1) * fine]

        @pl.when(end)
        def _():
            for sub in range(subs):
                item = pair * subs + sub
                hop_ref[near, item] = product[sub * fine : (sub + 1) * fine].astype(jnp.bfloat16)
                hop(near, item, inner).start()

    for pair in range(pairs):
        produce(pair, 0)
        produce(pair, 1)
        if pair:
            multiply(pair - 1)
    multiply(pairs - 1)

    def home(item):
        slot = all_ref.at[item // subs, core, item % subs]
        return remote(slot, slot, home_send, home_recv.at[item], "tensor", partner)

    def relay(item):
        @pl.when(jnp.logical_not(end))
        def _():
            hop(near, item, inner).wait_recv()
            hop_ref[near, item] = (part_ref[item] + land_ref[near, item].astype(jnp.float32)).astype(jnp.bfloat16)
            hop(near, item, inner).start()

    def close(item):
        hop(far, item, outer).wait_recv()
        running = part_ref[item] + land_ref[far, item].astype(jnp.float32)

        @pl.when(jnp.logical_not(end))
        def _():
            hop_ref[far, item] = running.astype(jnp.bfloat16)
            hop(far, item, outer).start()

        shared = running + land_ref[near, item].astype(jnp.float32)
        squares = jnp.mean(shared * shared, axis=1, keepdims=True)
        all_ref[item // subs, core, item % subs] = (shared * lax.rsqrt(squares + SCALE_EPS) * gain_ref[...]).astype(jnp.bfloat16)
        home(item).start()

    def finish(pair):
        for sub in range(subs):
            home(pair * subs + sub).wait_recv()
        gathered = all_ref[pair].reshape(2 * rows, columns)
        out_ref[2 * pair * rows : 2 * (pair + 1) * rows, :] = dot(gathered, mixer_ref[...]).astype(jnp.bfloat16)

    for item in range(count_of + LAG):
        if item < count_of:
            relay(item)
        item -= LAG
        if item >= 0:
            close(item)
            if item % subs == subs - 1 and item >= subs:
                finish(item // subs - 1)
    finish(pairs - 1)

    sent_later(count, *stats)
    sent_later(count, *states)
    swap.wait_send()
    remote(mate_ref, mate_ref, mate_send, mate_recv.at[0], "tensor", partner).wait_send()
    remote(hop_ref.at[0], land_ref.at[0], home_send, home_recv.at[0], "tensor", partner).wait_send()
    remote(hop_ref.at[0], land_ref.at[0], hop_send.at[near], hop_recv.at[0, 0], "tensor", inner).wait_send()

    @pl.when(jnp.logical_not(end))
    def _():
        remote(hop_ref.at[0], land_ref.at[0], hop_send.at[far], hop_recv.at[0, 0], "tensor", outer).wait_send()


def layer(tokens, retain, norm_gain, norm_bias, rate, angle, source, output, skip, weight, gain, mixer):
    length, channels = tokens.shape
    ndim = rate.shape[0]
    blocks = length // STEPS
    count = lax.axis_size("span")
    chips = lax.axis_size("tensor") // 2
    columns = weight.shape[1]
    pairs = length // (2 * ROWS)
    items = length // (2 * FINE)
    f32, bf16 = jnp.float32, jnp.bfloat16
    sems = pltpu.SemaphoreType.DMA
    hbm = pl.BlockSpec(memory_space=pltpu.HBM)
    operands = [
        tokens,
        retain.reshape(1, -1),
        norm_gain.reshape(1, -1),
        norm_bias.reshape(1, -1),
        rate,
        angle,
        source,
        output,
        skip.reshape(1, -1),
        gain.reshape(1, -1),
        weight,
        mixer,
    ]
    held = [pltpu.VMEM(a.shape, a.dtype) for a in operands[:10]]
    return pl.pallas_call(
        functools.partial(layer_kernel, count, chips),
        out_shape=pltpu.VMEM((length, mixer.shape[1]), bf16),
        in_specs=[hbm] * 12,
        out_specs=VMEM,
        scratch_shapes=held
        + [
            pltpu.VMEM((2,) + weight.shape, bf16),
            pltpu.VMEM(mixer.shape, bf16),
            pltpu.VMEM((8, channels), f32),
            pltpu.VMEM((count, 8, channels), f32),
            pltpu.VMEM((8, channels), f32),
            pltpu.VMEM((length, channels), f32),
            pltpu.VMEM((blocks, STEPS, channels), f32),
            pltpu.VMEM((blocks, STEPS, LANES), f32),
            pltpu.VMEM((2, STEPS + 1, ndim, channels), f32),
            pltpu.VMEM((2, ndim, channels), f32),
            pltpu.VMEM((2, ndim, channels), f32),
            pltpu.VMEM((2, ndim, channels), f32),
            pltpu.VMEM((2, ndim, STEPS, channels), f32),
            pltpu.VMEM((2, blocks, ndim, channels), f32),
            pltpu.VMEM((2 * ndim, channels), bf16),
            pltpu.VMEM((count, 2 * ndim, channels), bf16),
            pltpu.VMEM((length, channels), f32),
            pltpu.VMEM((pairs, 2, ROWS, channels), bf16),
            pltpu.VMEM((pairs, ROWS, channels), bf16),
            pltpu.VMEM((items, FINE, columns), f32),
            pltpu.VMEM((2, items, FINE, columns), bf16),
            pltpu.VMEM((2, items, FINE, columns), bf16),
            pltpu.VMEM((pairs, 2, ROWS // FINE, FINE, columns), bf16),
            sems((4,)),
            sems(()),
            sems((count - 1,)),
            sems(()),
            sems((count - 1,)),
            sems(()),
            sems(()),
            sems(()),
            sems((pairs,)),
            sems((2,)),
            sems((2, items)),
            sems(()),
            sems((items,)),
        ],
        compiler_params=pltpu.CompilerParams(collective_id=0, has_side_effects=True),
        name="layer",
    )(*operands)


def solution(mesh):
    in_specs = (
        P("span", "tensor"),
        P("span"),
        P("tensor"),
        P("tensor"),
        P(None, "tensor"),
        P(None, "tensor"),
        P(None, "tensor"),
        P(None, None, "tensor"),
        P("tensor"),
        P("tensor", None),
        P(),
        P(None, "tensor"),
    )
    return jax.shard_map(layer, mesh=mesh, in_specs=in_specs, out_specs=P("span", "tensor"), check_vma=False)
```

```python
import functools

import jax
import jax.numpy as jnp
from jax import lax
from jax.experimental import pallas as pl
from jax.experimental.pallas import tpu as pltpu
from jax.sharding import PartitionSpec as P

GROUP = 64
STEPS = 8
LANES = 128
ROWS = 32
FINE = 16
LAG = 5
ENTER = 256
UNROLL = 4
LEAVE = 256
NORM_EPS = 1e-05
SCALE_EPS = 1e-06

MESH = pl.DeviceIdType.MESH
VMEM = pl.BlockSpec(memory_space=pltpu.VMEM)


def dot(a, b):
    return jnp.dot(a, b, preferred_element_type=jnp.float32)


def pieces(values, count):
    out = []
    for _ in range(count):
        piece = values.astype(jnp.bfloat16)
        out.append(piece)
        values = values - piece.astype(jnp.float32)
    return out


def group_ones(channels):
    row = lax.broadcasted_iota(jnp.int32, (channels, channels), 0) // GROUP
    column = lax.broadcasted_iota(jnp.int32, (channels, channels), 1) // GROUP
    return (row == column).astype(jnp.bfloat16)


def remote(source, target, send_sem, recv_sem, axis, device):
    return pltpu.make_async_remote_copy(
        src_ref=source,
        dst_ref=target,
        send_sem=send_sem,
        recv_sem=recv_sem,
        device_id={axis: device},
        device_id_type=MESH,
    )


def to_later(count, source, landing, send_sem, recv_sem):
    me = lax.axis_index("span")
    for step in range(1, count):

        @pl.when(me + step < count)
        def _():
            remote(source, landing.at[me], send_sem, recv_sem, "span", me + step).start()


def from_earlier(count, source, landing, send_sem, recv_sem):
    me = lax.axis_index("span")
    for place in range(1, count):

        @pl.when(me == place)
        def _():
            here = landing.at[0:place]
            remote(here, here, send_sem, recv_sem, "span", 0).wait_recv()


def sent_later(count, source, landing, send_sem, recv_sem):
    me = lax.axis_index("span")
    for step in range(1, count):

        @pl.when(me + step < count)
        def _():
            remote(source, landing.at[me], send_sem, recv_sem, "span", me + step).wait_send()


def wide(column, width):
    return jnp.concatenate([column] * (width // LANES), axis=1)


def lanes_of(channels, width):
    return [slice(start, start + width) for start in range(0, channels, width)]


def layer_kernel(
    count,
    chips,
    tokens_hbm,
    retain_hbm,
    norm_gain_hbm,
    bias_hbm,
    rate_hbm,
    angle_hbm,
    input_hbm,
    output_hbm,
    skip_hbm,
    gain_hbm,
    weight_hbm,
    mixer_hbm,
    out_ref,
    tokens_ref,
    retain_ref,
    norm_gain_ref,
    bias_ref,
    rate_ref,
    angle_ref,
    input_ref,
    output_ref,
    skip_ref,
    gain_ref,
    weight_ref,
    mixer_ref,
    total_ref,
    totals_ref,
    before_ref,
    normed_ref,
    scaled_ref,
    prefix_ref,
    power_ref,
    unit_ref,
    whole_ref,
    carry_ref,
    read_ref,
    start_ref,
    state_ref,
    states_ref,
    ema_ref,
    active_ref,
    mate_ref,
    part_ref,
    hop_ref,
    land_ref,
    all_ref,
    load_sem,
    total_send,
    total_recv,
    state_send,
    state_recv,
    weight_send,
    weight_recv,
    mate_send,
    mate_recv,
    hop_send,
    hop_recv,
    home_send,
    home_recv,
):
    length, channels = tokens_ref.shape
    ndim = rate_ref.shape[0]
    blocks = length // STEPS
    pairs, _, subs, fine, columns = all_ref.shape
    rows = subs * fine
    count_of = pairs * subs
    span = lax.axis_index("span")
    me = lax.axis_index("tensor")
    core = lax.rem(me, 2)
    chip = lax.div(me, 2)
    partner = me + 1 - 2 * core
    left, right = chip > 0, chip < chips - 1
    near = jnp.where(2 * chip < chips, 0, 1)
    far = 1 - near
    inner, outer = me + 2 - 4 * near, me - 2 + 4 * near
    end = jnp.logical_or(chip == 0, chip == chips - 1)

    barrier = pltpu.get_barrier_semaphore()
    for step in range(1, count):
        pl.semaphore_signal(barrier, inc=1, device_id={"span": lax.rem(span + step, count)}, device_id_type=MESH)
    pl.semaphore_signal(barrier, inc=1, device_id={"tensor": partner}, device_id_type=MESH)

    @pl.when(left)
    def _():
        pl.semaphore_signal(barrier, inc=1, device_id={"tensor": me - 2}, device_id_type=MESH)

    @pl.when(right)
    def _():
        pl.semaphore_signal(barrier, inc=1, device_id={"tensor": me + 2}, device_id_type=MESH)

    moves = [
        (retain_hbm, retain_ref, 0),
        (tokens_hbm, tokens_ref, 1),
        (rate_hbm, rate_ref, 2),
        (angle_hbm, angle_ref, 2),
        (input_hbm, input_ref, 2),
        (output_hbm, output_ref, 2),
        (norm_gain_hbm, norm_gain_ref, 2),
        (bias_hbm, bias_ref, 2),
        (skip_hbm, skip_ref, 2),
        (gain_hbm, gain_ref, 2),
        (weight_hbm, weight_ref.at[0], 3),
        (mixer_hbm, mixer_ref, 3),
    ]
    loads = [pltpu.make_async_copy(source, target, load_sem.at[item]) for source, target, item in moves]
    for load in loads:
        load.start()

    row = lax.broadcasted_iota(jnp.int32, (length, length), 0)
    column = lax.broadcasted_iota(jnp.int32, (length, length), 1)
    ones = group_ones(channels)
    loads[0].wait()
    diagonal = jnp.where(row == column, jnp.broadcast_to(retain_ref[...], (length, length)), 0.0)
    keep = sum(dot(piece, jnp.ones((length, LANES), jnp.bfloat16)) for piece in pieces(diagonal, 3))
    kept = keep.reshape(blocks, STEPS, LANES)
    while kept.shape[0] > 1:
        half = kept.shape[0] // 2
        kept = kept[:half] * kept[half:]
    kept = kept[0]
    for by in (1, 2, 4):
        kept = kept * pltpu.roll(kept, by, 0)
    loads[1].wait()
    tokens = tokens_ref[...]
    values = tokens.astype(jnp.float32)
    total = jnp.sum(values, axis=0, keepdims=True)
    squares = jnp.sum(values * values, axis=0, keepdims=True)
    summed = jnp.concatenate([total, squares, jnp.zeros((6, channels), jnp.float32)], axis=0)
    summed = sum(dot(piece, ones) for piece in pieces(summed, 3))
    top = lax.broadcasted_iota(jnp.int32, (8, channels), 0) < 2
    total_ref[...] = jnp.where(top, summed, wide(kept, channels))
    pl.semaphore_wait(barrier, count + left.astype(jnp.int32) + right.astype(jnp.int32))
    stats = (total_ref, totals_ref, total_send, total_recv)
    to_later(count, *stats)
    swap = remote(weight_hbm, weight_ref.at[1], weight_send, weight_recv, "tensor", partner)
    swap.start()

    for load in loads[2:10]:
        load.wait()
    rate, angle = rate_ref[...], angle_ref[...]
    size = jnp.exp(-rate)
    turn_re = size * jnp.cos(angle)
    turn_im = size * jnp.sin(angle)
    weight = (1.0 - size) * input_ref[...]
    read_re = weight * output_ref[0]
    read_im = weight * output_ref[1]
    power_re, power_im = jnp.ones_like(rate), jnp.zeros_like(rate)
    lag_rows = []
    for lag in range(STEPS + 1):
        if lag < STEPS:
            lag_rows.append(jnp.sum(read_re * power_re - read_im * power_im, axis=0, keepdims=True))
        power_ref[0, lag] = power_re
        power_ref[1, lag] = power_im
        power_re, power_im = power_re * turn_re - power_im * turn_im, power_re * turn_im + power_im * turn_re
    unit_ref[0] = read_re * turn_re - read_im * turn_im
    unit_ref[1] = read_re * turn_im + read_im * turn_re
    whole = jnp.exp(-rate * length)
    whole_ref[0] = whole * jnp.cos(angle * length)
    whole_ref[1] = whole * jnp.sin(angle * length)
    step_row = lax.broadcasted_iota(jnp.int32, (STEPS, channels), 0)

    def table(part, carried):
        here = pl.ds(part, 1)
        re = jnp.broadcast_to(unit_ref[0, here, :], (STEPS, channels))
        im = jnp.broadcast_to(unit_ref[1, here, :], (STEPS, channels))
        for bit in (1, 2, 4):
            chosen = (step_row // bit) % 2 == 1
            by_re = jnp.where(chosen, jnp.broadcast_to(power_ref[0, bit, here, :], (STEPS, channels)), 1.0)
            by_im = jnp.where(chosen, jnp.broadcast_to(power_ref[1, bit, here, :], (STEPS, channels)), 0.0)
            re, im = re * by_re - im * by_im, re * by_im + im * by_re
        read_ref[0, part] = re
        read_ref[1, part] = im
        return carried

    lax.fori_loop(0, ndim, table, 0)

    sums = dot(tokens, ones)
    squares = sum(dot(piece, ones) for piece in pieces(values * values, 2))
    lower = (column <= row).astype(jnp.bfloat16)
    cum_sum = sum(dot(lower, piece) for piece in pieces(sums, 3))
    cum_sq = sum(dot(lower, piece) for piece in pieces(squares, 3))
    place_in = lax.broadcasted_iota(jnp.int32, (length, LANES), 0) % STEPS
    prefix = keep
    suffix = jnp.where(place_in < STEPS - 1, pltpu.roll(keep, length - 1, 0), 1.0)
    for by in (1, 2, 4):
        prefix = jnp.where(place_in >= by, prefix * pltpu.roll(prefix, by, 0), prefix)
        suffix = jnp.where(place_in + by < STEPS, suffix * pltpu.roll(suffix, length - by, 0), suffix)
    prefix_ref[...] = prefix.reshape(blocks, STEPS, LANES)
    position = lax.broadcasted_iota(jnp.int32, (length, LANES), 0)
    share = wide(1.0 / ((span * length + position + 1) * GROUP).astype(jnp.float32), channels)

    from_earlier(count, *stats)
    before_ref[...] = jnp.zeros((8, channels), jnp.float32)
    for other in range(count - 1):

        @pl.when(other < span)
        def _():
            before_ref[...] += totals_ref[other]

    average = (before_ref[0:1] + cum_sum) * share
    spread = (before_ref[1:2] + cum_sq) * share - average * average
    inverse = lax.rsqrt(spread + NORM_EPS)
    normed = (values - average) * inverse * norm_gain_ref[...] + bias_ref[...]
    normed_ref[...] = normed
    scaled_ref[...] = (normed * wide(suffix, channels)).reshape(blocks, STEPS, channels)

    width = min(ENTER, channels)
    for lanes in lanes_of(channels, width):
        powers = [(power_ref[0, lag, :, lanes], power_ref[1, lag, :, lanes]) for lag in range(STEPS + 1)]

        def enter(block, carried):
            re, im = carried
            start_ref[0, block, :, lanes] = re
            start_ref[1, block, :, lanes] = im
            factor = wide(prefix_ref[block, STEPS - 1 : STEPS, :], width)
            add_re = jnp.broadcast_to(scaled_ref[block, STEPS - 1 : STEPS, lanes], (ndim, width))
            add_im = None
            for step in reversed(range(STEPS - 1)):
                entry = scaled_ref[block, step : step + 1, lanes]
                by_re, by_im = powers[STEPS - 1 - step]
                add_re = add_re + by_re * entry
                add_im = by_im * entry if add_im is None else add_im + by_im * entry
            re, im = re * factor, im * factor
            by_re, by_im = powers[STEPS]
            return by_re * re - by_im * im + add_re, by_re * im + by_im * re + add_im

        zero = jnp.zeros((ndim, width), jnp.float32)
        re, im = lax.fori_loop(0, blocks, enter, (zero, zero), unroll=UNROLL)
        state_ref[0:ndim, lanes] = re.astype(state_ref.dtype)
        state_ref[ndim : 2 * ndim, lanes] = im.astype(state_ref.dtype)
    states = (state_ref, states_ref, state_send, state_recv)
    to_later(count, *states)

    for lanes in lanes_of(channels, LANES):
        reach = jnp.where(place_in >= 0, 1.0, 0.0)
        here = normed_ref[:, lanes]
        within = here * lag_rows[0][:, lanes]
        for lag in range(1, STEPS):
            reach = jnp.where(place_in >= lag, reach * (pltpu.roll(keep, lag - 1, 0) if lag > 1 else keep), 0.0)
            within = within + pltpu.roll(here, lag, 0) * (lag_rows[lag][:, lanes] * reach)
        ema_ref[:, lanes] = within + skip_ref[:, lanes] * here

    @pl.when(end)
    def _():
        land_ref[near] = jnp.zeros(land_ref.shape[1:], land_ref.dtype)

    loads[10].wait()
    loads[11].wait()
    swap.wait_recv()
    carry_ref[...] = jnp.zeros(carry_ref.shape, jnp.float32)
    from_earlier(count, *states)
    for other in range(count - 1):

        @pl.when(other < span)
        def _():
            kept = totals_ref[other, 2:3, :]
            re, im = carry_ref[0], carry_ref[1]
            by_re, by_im = whole_ref[0], whole_ref[1]
            carry_ref[0] = (by_re * re - by_im * im) * kept + states_ref[other, 0:ndim].astype(jnp.float32)
            carry_ref[1] = (by_re * im + by_im * re) * kept + states_ref[other, ndim : 2 * ndim].astype(jnp.float32)

    width = min(LEAVE, channels)
    inside = rows // STEPS

    def produce(pair, side):
        chunk = 2 * pair + side
        for lanes in lanes_of(channels, width):
            whole_re, whole_im = power_ref[0, STEPS, :, lanes], power_ref[1, STEPS, :, lanes]
            re, im = carry_ref[0, :, lanes], carry_ref[1, :, lanes]
            for block in range(chunk * inside, (chunk + 1) * inside):
                start_ref[0, block, :, lanes] += re
                start_ref[1, block, :, lanes] += im
                factor = wide(prefix_ref[block, STEPS - 1 : STEPS, :], width)
                re, im = (whole_re * re - whole_im * im) * factor, (whole_re * im + whole_im * re) * factor
            carry_ref[0, :, lanes] = re
            carry_ref[1, :, lanes] = im
            reads = [None] * inside
            for part in range(ndim):
                by_re, by_im = read_ref[0, part, :, lanes], read_ref[1, part, :, lanes]
                for spot in range(inside):
                    block = chunk * inside + spot
                    term = by_re * start_ref[0, block, part : part + 1, lanes] - by_im * start_ref[1, block, part : part + 1, lanes]
                    reads[spot] = term if reads[spot] is None else reads[spot] + term
            for spot in range(inside):
                here = slice((chunk * inside + spot) * STEPS, (chunk * inside + spot + 1) * STEPS)
                ema_ref[here, lanes] += reads[spot] * wide(prefix_ref[chunk * inside + spot], width)
        ema = ema_ref[chunk * rows : (chunk + 1) * rows, :]
        active_ref[pair, side] = (ema / (1.0 + jnp.exp(-ema))).astype(jnp.bfloat16)

        @pl.when(core != side)
        def _():
            remote(active_ref.at[pair, side], mate_ref.at[pair], mate_send, mate_recv.at[pair], "tensor", partner).start()

    def hop(way, item, target):
        return remote(hop_ref.at[way, item], land_ref.at[way, item], hop_send.at[way], hop_recv.at[way, item], "tensor", target)

    def multiply(pair):
        remote(active_ref.at[pair, 1 - core], mate_ref.at[pair], mate_send, mate_recv.at[pair], "tensor", partner).wait_recv()
        product = dot(active_ref[pair, core], weight_ref[0]) + dot(mate_ref[pair], weight_ref[1])
        for sub in range(subs):
            part_ref[pair * subs + sub] = product[sub * fine : (sub + 1) * fine]

        @pl.when(end)
        def _():
            for sub in range(subs):
                item = pair * subs + sub
                hop_ref[near, item] = product[sub * fine : (sub + 1) * fine].astype(jnp.bfloat16)
                hop(near, item, inner).start()

    for pair in range(pairs):
        produce(pair, 0)
        produce(pair, 1)

        @pl.when(core == 0)
        def _():
            multiply(pair)

    @pl.when(core == 1)
    def _():
        for pair in range(pairs):
            multiply(pair)

    def home(item):
        slot = all_ref.at[item // subs, core, item % subs]
        return remote(slot, slot, home_send, home_recv.at[item // subs], "tensor", partner)

    def relay(item):
        @pl.when(jnp.logical_not(end))
        def _():
            hop(near, item, inner).wait_recv()
            hop_ref[near, item] = (part_ref[item] + land_ref[near, item].astype(jnp.float32)).astype(jnp.bfloat16)
            hop(near, item, inner).start()

    def close(item):
        hop(far, item, outer).wait_recv()
        running = part_ref[item] + land_ref[far, item].astype(jnp.float32)

        @pl.when(jnp.logical_not(end))
        def _():
            hop_ref[far, item] = running.astype(jnp.bfloat16)
            hop(far, item, outer).start()

        shared = running + land_ref[near, item].astype(jnp.float32)
        squares = jnp.mean(shared * shared, axis=1, keepdims=True)
        all_ref[item // subs, core, item % subs] = (shared * lax.rsqrt(squares + SCALE_EPS) * gain_ref[...]).astype(jnp.bfloat16)
        home(item).start()

    def finish(pair):
        slot = all_ref.at[pair, core]
        remote(slot, slot, home_send, home_recv.at[pair], "tensor", partner).wait_recv()
        gathered = all_ref[pair].reshape(2 * rows, columns)
        out_ref[2 * pair * rows : 2 * (pair + 1) * rows, :] = dot(gathered, mixer_ref[...]).astype(jnp.bfloat16)

    for item in range(count_of + LAG):
        if item < count_of:
            relay(item)
        item -= LAG
        if item >= 0:
            close(item)
            if item % subs == subs - 1 and item >= subs:
                finish(item // subs - 1)
    finish(pairs - 1)

    sent_later(count, *stats)
    sent_later(count, *states)
    swap.wait_send()
    remote(mate_ref, mate_ref, mate_send, mate_recv.at[0], "tensor", partner).wait_send()
    remote(hop_ref.at[0], land_ref.at[0], home_send, home_recv.at[0], "tensor", partner).wait_send()
    remote(hop_ref.at[0], land_ref.at[0], hop_send.at[near], hop_recv.at[0, 0], "tensor", inner).wait_send()

    @pl.when(jnp.logical_not(end))
    def _():
        remote(hop_ref.at[0], land_ref.at[0], hop_send.at[far], hop_recv.at[0, 0], "tensor", outer).wait_send()


def layer(tokens, retain, norm_gain, norm_bias, rate, angle, source, output, skip, weight, gain, mixer):
    length, channels = tokens.shape
    ndim = rate.shape[0]
    blocks = length // STEPS
    count = lax.axis_size("span")
    chips = lax.axis_size("tensor") // 2
    columns = weight.shape[1]
    pairs = length // (2 * ROWS)
    items = length // (2 * FINE)
    f32, bf16 = jnp.float32, jnp.bfloat16
    sems = pltpu.SemaphoreType.DMA
    hbm = pl.BlockSpec(memory_space=pltpu.HBM)
    operands = [
        tokens,
        retain.reshape(1, -1),
        norm_gain.reshape(1, -1),
        norm_bias.reshape(1, -1),
        rate,
        angle,
        source,
        output,
        skip.reshape(1, -1),
        gain.reshape(1, -1),
        weight,
        mixer,
    ]
    held = [pltpu.VMEM(a.shape, a.dtype) for a in operands[:10]]
    return pl.pallas_call(
        functools.partial(layer_kernel, count, chips),
        out_shape=pltpu.VMEM((length, mixer.shape[1]), bf16),
        in_specs=[hbm] * 12,
        out_specs=VMEM,
        scratch_shapes=held
        + [
            pltpu.VMEM((2,) + weight.shape, bf16),
            pltpu.VMEM(mixer.shape, bf16),
            pltpu.VMEM((8, channels), f32),
            pltpu.VMEM((count, 8, channels), f32),
            pltpu.VMEM((8, channels), f32),
            pltpu.VMEM((length, channels), f32),
            pltpu.VMEM((blocks, STEPS, channels), f32),
            pltpu.VMEM((blocks, STEPS, LANES), f32),
            pltpu.VMEM((2, STEPS + 1, ndim, channels), f32),
            pltpu.VMEM((2, ndim, channels), f32),
            pltpu.VMEM((2, ndim, channels), f32),
            pltpu.VMEM((2, ndim, channels), f32),
            pltpu.VMEM((2, ndim, STEPS, channels), f32),
            pltpu.VMEM((2, blocks, ndim, channels), f32),
            pltpu.VMEM((2 * ndim, channels), bf16),
            pltpu.VMEM((count, 2 * ndim, channels), bf16),
            pltpu.VMEM((length, channels), f32),
            pltpu.VMEM((pairs, 2, ROWS, channels), bf16),
            pltpu.VMEM((pairs, ROWS, channels), bf16),
            pltpu.VMEM((items, FINE, columns), f32),
            pltpu.VMEM((2, items, FINE, columns), bf16),
            pltpu.VMEM((2, items, FINE, columns), bf16),
            pltpu.VMEM((pairs, 2, ROWS // FINE, FINE, columns), bf16),
            sems((4,)),
            sems(()),
            sems(()),
            sems(()),
            sems(()),
            sems(()),
            sems(()),
            sems(()),
            sems((pairs,)),
            sems((2,)),
            sems((2, items)),
            sems(()),
            sems((pairs,)),
        ],
        compiler_params=pltpu.CompilerParams(collective_id=0, has_side_effects=True),
        name="layer",
    )(*operands)


def solution(mesh):
    in_specs = (
        P("span", "tensor"),
        P("span"),
        P("tensor"),
        P("tensor"),
        P(None, "tensor"),
        P(None, "tensor"),
        P(None, "tensor"),
        P(None, None, "tensor"),
        P("tensor"),
        P("tensor", None),
        P(),
        P(None, "tensor"),
    )
    return jax.shard_map(layer, mesh=mesh, in_specs=in_specs, out_specs=P("span", "tensor"), check_vma=False)
```

```python
import functools

import jax
import jax.numpy as jnp
from jax import lax
from jax.experimental import pallas as pl
from jax.experimental.pallas import tpu as pltpu
from jax.sharding import PartitionSpec as P

GROUP = 64
STEPS = 8
LANES = 128
ROWS = 32
FINE = 16
PARTS = 2
LAG = 10
ENTER = 256
UNROLL = 4
LEAVE = 256
NORM_EPS = 1e-05
SCALE_EPS = 1e-06

MESH = pl.DeviceIdType.MESH
VMEM = pl.BlockSpec(memory_space=pltpu.VMEM)


def dot(a, b):
    return jnp.dot(a, b, preferred_element_type=jnp.float32)


def pieces(values, count):
    out = []
    for _ in range(count):
        piece = values.astype(jnp.bfloat16)
        out.append(piece)
        values = values - piece.astype(jnp.float32)
    return out


def group_ones(channels):
    row = lax.broadcasted_iota(jnp.int32, (channels, channels), 0) // GROUP
    column = lax.broadcasted_iota(jnp.int32, (channels, channels), 1) // GROUP
    return (row == column).astype(jnp.bfloat16)


def remote(source, target, send_sem, recv_sem, axis, device):
    return pltpu.make_async_remote_copy(
        src_ref=source,
        dst_ref=target,
        send_sem=send_sem,
        recv_sem=recv_sem,
        device_id={axis: device},
        device_id_type=MESH,
    )


def to_later(count, source, landing, send_sem, recv_sem):
    me = lax.axis_index("span")
    for step in range(1, count):

        @pl.when(me + step < count)
        def _():
            remote(source, landing.at[me], send_sem, recv_sem, "span", me + step).start()


def from_earlier(count, source, landing, send_sem, recv_sem):
    me = lax.axis_index("span")
    for place in range(1, count):

        @pl.when(me == place)
        def _():
            here = landing.at[0:place]
            remote(here, here, send_sem, recv_sem, "span", 0).wait_recv()


def sent_later(count, source, landing, send_sem, recv_sem):
    me = lax.axis_index("span")
    for step in range(1, count):

        @pl.when(me + step < count)
        def _():
            remote(source, landing.at[me], send_sem, recv_sem, "span", me + step).wait_send()


def wide(column, width):
    return jnp.concatenate([column] * (width // LANES), axis=1)


def lanes_of(channels, width):
    return [slice(start, start + width) for start in range(0, channels, width)]


def layer_kernel(
    count,
    chips,
    tokens_hbm,
    retain_hbm,
    norm_gain_hbm,
    bias_hbm,
    rate_hbm,
    angle_hbm,
    input_hbm,
    output_hbm,
    skip_hbm,
    gain_hbm,
    weight_hbm,
    mixer_hbm,
    out_ref,
    tokens_ref,
    retain_ref,
    norm_gain_ref,
    bias_ref,
    rate_ref,
    angle_ref,
    input_ref,
    output_ref,
    skip_ref,
    gain_ref,
    weight_ref,
    mixer_ref,
    total_ref,
    totals_ref,
    before_ref,
    normed_ref,
    scaled_ref,
    prefix_ref,
    power_ref,
    unit_ref,
    whole_ref,
    carry_ref,
    read_ref,
    start_ref,
    state_ref,
    states_ref,
    ema_ref,
    active_ref,
    mate_ref,
    part_ref,
    hop_ref,
    land_ref,
    all_ref,
    load_sem,
    total_send,
    total_recv,
    state_send,
    state_recv,
    weight_send,
    weight_recv,
    mate_send,
    mate_recv,
    hop_send,
    hop_recv,
    home_send,
    home_recv,
):
    length, channels = tokens_ref.shape
    ndim = rate_ref.shape[0]
    blocks = length // STEPS
    pairs, _, subs, fine, columns = all_ref.shape
    rows = subs * fine
    piece_columns = columns // PARTS
    count_of = pairs * subs * PARTS
    span = lax.axis_index("span")
    me = lax.axis_index("tensor")
    core = lax.rem(me, 2)
    chip = lax.div(me, 2)
    partner = me + 1 - 2 * core
    left, right = chip > 0, chip < chips - 1
    near = jnp.where(2 * chip < chips, 0, 1)
    far = 1 - near
    inner, outer = me + 2 - 4 * near, me - 2 + 4 * near
    end = jnp.logical_or(chip == 0, chip == chips - 1)

    barrier = pltpu.get_barrier_semaphore()
    for step in range(1, count):
        pl.semaphore_signal(barrier, inc=1, device_id={"span": lax.rem(span + step, count)}, device_id_type=MESH)
    pl.semaphore_signal(barrier, inc=1, device_id={"tensor": partner}, device_id_type=MESH)

    @pl.when(left)
    def _():
        pl.semaphore_signal(barrier, inc=1, device_id={"tensor": me - 2}, device_id_type=MESH)

    @pl.when(right)
    def _():
        pl.semaphore_signal(barrier, inc=1, device_id={"tensor": me + 2}, device_id_type=MESH)

    moves = [
        (retain_hbm, retain_ref, 0),
        (tokens_hbm, tokens_ref, 1),
        (rate_hbm, rate_ref, 2),
        (angle_hbm, angle_ref, 2),
        (input_hbm, input_ref, 2),
        (output_hbm, output_ref, 2),
        (norm_gain_hbm, norm_gain_ref, 2),
        (bias_hbm, bias_ref, 2),
        (skip_hbm, skip_ref, 2),
        (gain_hbm, gain_ref, 2),
        (weight_hbm, weight_ref.at[0], 3),
        (mixer_hbm, mixer_ref, 3),
    ]
    loads = [pltpu.make_async_copy(source, target, load_sem.at[item]) for source, target, item in moves]
    for load in loads:
        load.start()

    row = lax.broadcasted_iota(jnp.int32, (length, length), 0)
    column = lax.broadcasted_iota(jnp.int32, (length, length), 1)
    ones = group_ones(channels)
    loads[0].wait()
    diagonal = jnp.where(row == column, jnp.broadcast_to(retain_ref[...], (length, length)), 0.0)
    keep = sum(dot(piece, jnp.ones((length, LANES), jnp.bfloat16)) for piece in pieces(diagonal, 3))
    kept = keep.reshape(blocks, STEPS, LANES)
    while kept.shape[0] > 1:
        half = kept.shape[0] // 2
        kept = kept[:half] * kept[half:]
    kept = kept[0]
    for by in (1, 2, 4):
        kept = kept * pltpu.roll(kept, by, 0)
    loads[1].wait()
    tokens = tokens_ref[...]
    values = tokens.astype(jnp.float32)
    total = jnp.sum(values, axis=0, keepdims=True)
    squares = jnp.sum(values * values, axis=0, keepdims=True)
    summed = jnp.concatenate([total, squares, jnp.zeros((6, channels), jnp.float32)], axis=0)
    summed = sum(dot(piece, ones) for piece in pieces(summed, 3))
    top = lax.broadcasted_iota(jnp.int32, (8, channels), 0) < 2
    total_ref[...] = jnp.where(top, summed, wide(kept, channels))
    pl.semaphore_wait(barrier, count + left.astype(jnp.int32) + right.astype(jnp.int32))
    stats = (total_ref, totals_ref, total_send, total_recv)
    to_later(count, *stats)
    swap = remote(weight_hbm, weight_ref.at[1], weight_send, weight_recv, "tensor", partner)
    swap.start()

    for load in loads[2:10]:
        load.wait()
    rate, angle = rate_ref[...], angle_ref[...]
    size = jnp.exp(-rate)
    turn_re = size * jnp.cos(angle)
    turn_im = size * jnp.sin(angle)
    weight = (1.0 - size) * input_ref[...]
    read_re = weight * output_ref[0]
    read_im = weight * output_ref[1]
    power_re, power_im = jnp.ones_like(rate), jnp.zeros_like(rate)
    lag_rows = []
    for lag in range(STEPS + 1):
        if lag < STEPS:
            lag_rows.append(jnp.sum(read_re * power_re - read_im * power_im, axis=0, keepdims=True))
        power_ref[0, lag] = power_re
        power_ref[1, lag] = power_im
        power_re, power_im = power_re * turn_re - power_im * turn_im, power_re * turn_im + power_im * turn_re
    unit_ref[0] = read_re * turn_re - read_im * turn_im
    unit_ref[1] = read_re * turn_im + read_im * turn_re
    whole = jnp.exp(-rate * length)
    whole_ref[0] = whole * jnp.cos(angle * length)
    whole_ref[1] = whole * jnp.sin(angle * length)
    step_row = lax.broadcasted_iota(jnp.int32, (STEPS, channels), 0)

    def table(part, carried):
        here = pl.ds(part, 1)
        re = jnp.broadcast_to(unit_ref[0, here, :], (STEPS, channels))
        im = jnp.broadcast_to(unit_ref[1, here, :], (STEPS, channels))
        for bit in (1, 2, 4):
            chosen = (step_row // bit) % 2 == 1
            by_re = jnp.where(chosen, jnp.broadcast_to(power_ref[0, bit, here, :], (STEPS, channels)), 1.0)
            by_im = jnp.where(chosen, jnp.broadcast_to(power_ref[1, bit, here, :], (STEPS, channels)), 0.0)
            re, im = re * by_re - im * by_im, re * by_im + im * by_re
        read_ref[0, part] = re
        read_ref[1, part] = im
        return carried

    lax.fori_loop(0, ndim, table, 0)

    sums = dot(tokens, ones)
    squares = sum(dot(piece, ones) for piece in pieces(values * values, 2))
    lower = (column <= row).astype(jnp.bfloat16)
    cum_sum = sum(dot(lower, piece) for piece in pieces(sums, 3))
    cum_sq = sum(dot(lower, piece) for piece in pieces(squares, 3))
    place_in = lax.broadcasted_iota(jnp.int32, (length, LANES), 0) % STEPS
    prefix = keep
    suffix = jnp.where(place_in < STEPS - 1, pltpu.roll(keep, length - 1, 0), 1.0)
    for by in (1, 2, 4):
        prefix = jnp.where(place_in >= by, prefix * pltpu.roll(prefix, by, 0), prefix)
        suffix = jnp.where(place_in + by < STEPS, suffix * pltpu.roll(suffix, length - by, 0), suffix)
    prefix_ref[...] = prefix.reshape(blocks, STEPS, LANES)
    position = lax.broadcasted_iota(jnp.int32, (length, LANES), 0)
    share = wide(1.0 / ((span * length + position + 1) * GROUP).astype(jnp.float32), channels)

    from_earlier(count, *stats)
    before_ref[...] = jnp.zeros((8, channels), jnp.float32)
    for other in range(count - 1):

        @pl.when(other < span)
        def _():
            before_ref[...] += totals_ref[other]

    average = (before_ref[0:1] + cum_sum) * share
    spread = (before_ref[1:2] + cum_sq) * share - average * average
    inverse = lax.rsqrt(spread + NORM_EPS)
    normed = (values - average) * inverse * norm_gain_ref[...] + bias_ref[...]
    normed_ref[...] = normed
    scaled_ref[...] = (normed * wide(suffix, channels)).reshape(blocks, STEPS, channels)

    width = min(ENTER, channels)
    for lanes in lanes_of(channels, width):
        powers = [(power_ref[0, lag, :, lanes], power_ref[1, lag, :, lanes]) for lag in range(STEPS + 1)]

        def enter(block, carried):
            re, im = carried
            start_ref[0, block, :, lanes] = re
            start_ref[1, block, :, lanes] = im
            factor = wide(prefix_ref[block, STEPS - 1 : STEPS, :], width)
            add_re = jnp.broadcast_to(scaled_ref[block, STEPS - 1 : STEPS, lanes], (ndim, width))
            add_im = None
            for step in reversed(range(STEPS - 1)):
                entry = scaled_ref[block, step : step + 1, lanes]
                by_re, by_im = powers[STEPS - 1 - step]
                add_re = add_re + by_re * entry
                add_im = by_im * entry if add_im is None else add_im + by_im * entry
            re, im = re * factor, im * factor
            by_re, by_im = powers[STEPS]
            return by_re * re - by_im * im + add_re, by_re * im + by_im * re + add_im

        zero = jnp.zeros((ndim, width), jnp.float32)
        re, im = lax.fori_loop(0, blocks, enter, (zero, zero), unroll=UNROLL)
        state_ref[0:ndim, lanes] = re.astype(state_ref.dtype)
        state_ref[ndim : 2 * ndim, lanes] = im.astype(state_ref.dtype)
    states = (state_ref, states_ref, state_send, state_recv)
    to_later(count, *states)

    for lanes in lanes_of(channels, LANES):
        reach = jnp.where(place_in >= 0, 1.0, 0.0)
        here = normed_ref[:, lanes]
        within = here * lag_rows[0][:, lanes]
        for lag in range(1, STEPS):
            reach = jnp.where(place_in >= lag, reach * (pltpu.roll(keep, lag - 1, 0) if lag > 1 else keep), 0.0)
            within = within + pltpu.roll(here, lag, 0) * (lag_rows[lag][:, lanes] * reach)
        ema_ref[:, lanes] = within + skip_ref[:, lanes] * here

    @pl.when(end)
    def _():
        land_ref[near] = jnp.zeros(land_ref.shape[1:], land_ref.dtype)

    loads[10].wait()
    loads[11].wait()
    swap.wait_recv()
    carry_ref[...] = jnp.zeros(carry_ref.shape, jnp.float32)
    from_earlier(count, *states)
    for other in range(count - 1):

        @pl.when(other < span)
        def _():
            kept = totals_ref[other, 2:3, :]
            re, im = carry_ref[0], carry_ref[1]
            by_re, by_im = whole_ref[0], whole_ref[1]
            carry_ref[0] = (by_re * re - by_im * im) * kept + states_ref[other, 0:ndim].astype(jnp.float32)
            carry_ref[1] = (by_re * im + by_im * re) * kept + states_ref[other, ndim : 2 * ndim].astype(jnp.float32)

    width = min(LEAVE, channels)
    inside = rows // STEPS

    def produce(pair, side):
        chunk = 2 * pair + side
        for lanes in lanes_of(channels, width):
            whole_re, whole_im = power_ref[0, STEPS, :, lanes], power_ref[1, STEPS, :, lanes]
            re, im = carry_ref[0, :, lanes], carry_ref[1, :, lanes]
            for block in range(chunk * inside, (chunk + 1) * inside):
                start_ref[0, block, :, lanes] += re
                start_ref[1, block, :, lanes] += im
                factor = wide(prefix_ref[block, STEPS - 1 : STEPS, :], width)
                re, im = (whole_re * re - whole_im * im) * factor, (whole_re * im + whole_im * re) * factor
            carry_ref[0, :, lanes] = re
            carry_ref[1, :, lanes] = im
            reads = [None] * inside
            for part in range(ndim):
                by_re, by_im = read_ref[0, part, :, lanes], read_ref[1, part, :, lanes]
                for spot in range(inside):
                    block = chunk * inside + spot
                    term = by_re * start_ref[0, block, part : part + 1, lanes] - by_im * start_ref[1, block, part : part + 1, lanes]
                    reads[spot] = term if reads[spot] is None else reads[spot] + term
            for spot in range(inside):
                here = slice((chunk * inside + spot) * STEPS, (chunk * inside + spot + 1) * STEPS)
                ema_ref[here, lanes] += reads[spot] * wide(prefix_ref[chunk * inside + spot], width)
        ema = ema_ref[chunk * rows : (chunk + 1) * rows, :]
        active_ref[pair, side] = (ema / (1.0 + jnp.exp(-ema))).astype(jnp.bfloat16)

        @pl.when(core != side)
        def _():
            remote(active_ref.at[pair, side], mate_ref.at[pair], mate_send, mate_recv.at[pair], "tensor", partner).start()

    def hop(way, item, target):
        return remote(hop_ref.at[way, item], land_ref.at[way, item], hop_send.at[way], hop_recv.at[way, item], "tensor", target)

    def multiply(pair):
        remote(active_ref.at[pair, 1 - core], mate_ref.at[pair], mate_send, mate_recv.at[pair], "tensor", partner).wait_recv()
        product = dot(active_ref[pair, core], weight_ref[0]) + dot(mate_ref[pair], weight_ref[1])
        cuts = [
            product[sub * fine : (sub + 1) * fine, lanes]
            for sub in range(subs)
            for lanes in lanes_of(columns, piece_columns)
        ]
        for spot, cut in enumerate(cuts):
            part_ref[pair * subs * PARTS + spot] = cut

        @pl.when(end)
        def _():
            for spot, cut in enumerate(cuts):
                item = pair * subs * PARTS + spot
                hop_ref[near, item] = cut.astype(jnp.bfloat16)
                hop(near, item, inner).start()

    for pair in range(pairs):
        produce(pair, 0)
        produce(pair, 1)

        @pl.when(core == 0)
        def _():
            multiply(pair)

    @pl.when(core == 1)
    def _():
        for pair in range(pairs):
            multiply(pair)

    def home(item):
        slot = all_ref.at[item // subs, core, item % subs]
        return remote(slot, slot, home_send, home_recv.at[item // subs], "tensor", partner)

    def relay(item):
        @pl.when(jnp.logical_not(end))
        def _():
            hop(near, item, inner).wait_recv()
            hop_ref[near, item] = (part_ref[item] + land_ref[near, item].astype(jnp.float32)).astype(jnp.bfloat16)
            hop(near, item, inner).start()

    def close(item):
        hop(far, item, outer).wait_recv()
        running = part_ref[item] + land_ref[far, item].astype(jnp.float32)

        @pl.when(jnp.logical_not(end))
        def _():
            hop_ref[far, item] = running.astype(jnp.bfloat16)
            hop(far, item, outer).start()

        return running + land_ref[near, item].astype(jnp.float32)

    def settle(block, halves):
        squares = sum(jnp.sum(half * half, axis=1, keepdims=True) for half in halves) / columns
        scale = lax.rsqrt(squares + SCALE_EPS)
        for half, lanes in zip(halves, lanes_of(columns, piece_columns)):
            all_ref[block // subs, core, block % subs, :, lanes] = (half * scale * gain_ref[:, lanes]).astype(jnp.bfloat16)
        home(block).start()

    def finish(pair):
        slot = all_ref.at[pair, core]
        remote(slot, slot, home_send, home_recv.at[pair], "tensor", partner).wait_recv()
        gathered = all_ref[pair].reshape(2 * rows, columns)
        out_ref[2 * pair * rows : 2 * (pair + 1) * rows, :] = dot(gathered, mixer_ref[...]).astype(jnp.bfloat16)

    held = []
    for item in range(count_of + LAG):
        if item < count_of:
            relay(item)
        item -= LAG
        if item >= 0:
            held.append(close(item))
            if len(held) == PARTS:
                block = item // PARTS
                settle(block, held)
                held = []
                if block % subs == subs - 1 and block >= subs:
                    finish(block // subs - 1)
    finish(pairs - 1)

    sent_later(count, *stats)
    sent_later(count, *states)
    swap.wait_send()
    remote(mate_ref, mate_ref, mate_send, mate_recv.at[0], "tensor", partner).wait_send()
    remote(hop_ref.at[0], land_ref.at[0], home_send, home_recv.at[0], "tensor", partner).wait_send()
    remote(hop_ref.at[0], land_ref.at[0], hop_send.at[near], hop_recv.at[0, 0], "tensor", inner).wait_send()

    @pl.when(jnp.logical_not(end))
    def _():
        remote(hop_ref.at[0], land_ref.at[0], hop_send.at[far], hop_recv.at[0, 0], "tensor", outer).wait_send()


def layer(tokens, retain, norm_gain, norm_bias, rate, angle, source, output, skip, weight, gain, mixer):
    length, channels = tokens.shape
    ndim = rate.shape[0]
    blocks = length // STEPS
    count = lax.axis_size("span")
    chips = lax.axis_size("tensor") // 2
    columns = weight.shape[1]
    pairs = length // (2 * ROWS)
    items = PARTS * length // (2 * FINE)
    f32, bf16 = jnp.float32, jnp.bfloat16
    sems = pltpu.SemaphoreType.DMA
    hbm = pl.BlockSpec(memory_space=pltpu.HBM)
    operands = [
        tokens,
        retain.reshape(1, -1),
        norm_gain.reshape(1, -1),
        norm_bias.reshape(1, -1),
        rate,
        angle,
        source,
        output,
        skip.reshape(1, -1),
        gain.reshape(1, -1),
        weight,
        mixer,
    ]
    held = [pltpu.VMEM(a.shape, a.dtype) for a in operands[:10]]
    return pl.pallas_call(
        functools.partial(layer_kernel, count, chips),
        out_shape=pltpu.VMEM((length, mixer.shape[1]), bf16),
        in_specs=[hbm] * 12,
        out_specs=VMEM,
        scratch_shapes=held
        + [
            pltpu.VMEM((2,) + weight.shape, bf16),
            pltpu.VMEM(mixer.shape, bf16),
            pltpu.VMEM((8, channels), f32),
            pltpu.VMEM((count, 8, channels), f32),
            pltpu.VMEM((8, channels), f32),
            pltpu.VMEM((length, channels), f32),
            pltpu.VMEM((blocks, STEPS, channels), f32),
            pltpu.VMEM((blocks, STEPS, LANES), f32),
            pltpu.VMEM((2, STEPS + 1, ndim, channels), f32),
            pltpu.VMEM((2, ndim, channels), f32),
            pltpu.VMEM((2, ndim, channels), f32),
            pltpu.VMEM((2, ndim, channels), f32),
            pltpu.VMEM((2, ndim, STEPS, channels), f32),
            pltpu.VMEM((2, blocks, ndim, channels), f32),
            pltpu.VMEM((2 * ndim, channels), bf16),
            pltpu.VMEM((count, 2 * ndim, channels), bf16),
            pltpu.VMEM((length, channels), f32),
            pltpu.VMEM((pairs, 2, ROWS, channels), bf16),
            pltpu.VMEM((pairs, ROWS, channels), bf16),
            pltpu.VMEM((items, FINE, columns // PARTS), f32),
            pltpu.VMEM((2, items, FINE, columns // PARTS), bf16),
            pltpu.VMEM((2, items, FINE, columns // PARTS), bf16),
            pltpu.VMEM((pairs, 2, ROWS // FINE, FINE, columns), bf16),
            sems((4,)),
            sems(()),
            sems(()),
            sems(()),
            sems(()),
            sems(()),
            sems(()),
            sems(()),
            sems((pairs,)),
            sems((2,)),
            sems((2, items)),
            sems(()),
            sems((pairs,)),
        ],
        compiler_params=pltpu.CompilerParams(collective_id=0, has_side_effects=True),
        name="layer",
    )(*operands)


def solution(mesh):
    in_specs = (
        P("span", "tensor"),
        P("span"),
        P("tensor"),
        P("tensor"),
        P(None, "tensor"),
        P(None, "tensor"),
        P(None, "tensor"),
        P(None, None, "tensor"),
        P("tensor"),
        P("tensor", None),
        P(),
        P(None, "tensor"),
    )
    return jax.shard_map(layer, mesh=mesh, in_specs=in_specs, out_specs=P("span", "tensor"), check_vma=False)
```

```python
import functools

import jax
import jax.numpy as jnp
from jax import lax
from jax.experimental import pallas as pl
from jax.experimental.pallas import tpu as pltpu
from jax.sharding import PartitionSpec as P

GROUP = 64
STEPS = 8
LANES = 128
ROWS = 32
FINE = 16
PARTS = 2
LAG = 12
ENTER = 256
UNROLL = 8
LEAVE = 256
NORM_EPS = 1e-05
SCALE_EPS = 1e-06

MESH = pl.DeviceIdType.MESH
VMEM = pl.BlockSpec(memory_space=pltpu.VMEM)


def dot(a, b):
    return jnp.dot(a, b, preferred_element_type=jnp.float32)


def pieces(values, count):
    out = []
    for _ in range(count):
        piece = values.astype(jnp.bfloat16)
        out.append(piece)
        values = values - piece.astype(jnp.float32)
    return out


def group_ones(channels):
    row = lax.broadcasted_iota(jnp.int32, (channels, channels), 0) // GROUP
    column = lax.broadcasted_iota(jnp.int32, (channels, channels), 1) // GROUP
    return (row == column).astype(jnp.bfloat16)


def remote(source, target, send_sem, recv_sem, axis, device):
    return pltpu.make_async_remote_copy(
        src_ref=source,
        dst_ref=target,
        send_sem=send_sem,
        recv_sem=recv_sem,
        device_id={axis: device},
        device_id_type=MESH,
    )


def to_later(count, source, landing, send_sem, recv_sem):
    me = lax.axis_index("span")
    for step in range(1, count):

        @pl.when(me + step < count)
        def _():
            remote(source, landing.at[me], send_sem, recv_sem, "span", me + step).start()


def from_earlier(count, source, landing, send_sem, recv_sem):
    me = lax.axis_index("span")
    for place in range(1, count):

        @pl.when(me == place)
        def _():
            here = landing.at[0:place]
            remote(here, here, send_sem, recv_sem, "span", 0).wait_recv()


def sent_later(count, source, landing, send_sem, recv_sem):
    me = lax.axis_index("span")
    for step in range(1, count):

        @pl.when(me + step < count)
        def _():
            remote(source, landing.at[me], send_sem, recv_sem, "span", me + step).wait_send()


def wide(column, width):
    return jnp.concatenate([column] * (width // LANES), axis=1)


def lanes_of(channels, width):
    return [slice(start, start + width) for start in range(0, channels, width)]


def layer_kernel(
    count,
    chips,
    tokens_hbm,
    retain_hbm,
    norm_gain_hbm,
    bias_hbm,
    rate_hbm,
    angle_hbm,
    input_hbm,
    output_hbm,
    skip_hbm,
    gain_hbm,
    weight_hbm,
    mixer_hbm,
    out_ref,
    tokens_ref,
    retain_ref,
    norm_gain_ref,
    bias_ref,
    rate_ref,
    angle_ref,
    input_ref,
    output_ref,
    skip_ref,
    gain_ref,
    weight_ref,
    mixer_ref,
    total_ref,
    totals_ref,
    before_ref,
    normed_ref,
    scaled_ref,
    prefix_ref,
    power_ref,
    unit_ref,
    whole_ref,
    carry_ref,
    read_ref,
    start_ref,
    state_ref,
    states_ref,
    ema_ref,
    active_ref,
    mate_ref,
    part_ref,
    hop_ref,
    land_ref,
    all_ref,
    load_sem,
    total_send,
    total_recv,
    state_send,
    state_recv,
    weight_send,
    weight_recv,
    mate_send,
    mate_recv,
    hop_send,
    hop_recv,
    home_send,
    home_recv,
):
    length, channels = tokens_ref.shape
    ndim = rate_ref.shape[0]
    blocks = length // STEPS
    pairs, _, subs, fine, columns = all_ref.shape
    rows = subs * fine
    piece_columns = columns // PARTS
    count_of = pairs * subs * PARTS
    span = lax.axis_index("span")
    me = lax.axis_index("tensor")
    core = lax.rem(me, 2)
    chip = lax.div(me, 2)
    partner = me + 1 - 2 * core
    left, right = chip > 0, chip < chips - 1
    near = jnp.where(2 * chip < chips, 0, 1)
    far = 1 - near
    inner, outer = me + 2 - 4 * near, me - 2 + 4 * near
    end = jnp.logical_or(chip == 0, chip == chips - 1)

    barrier = pltpu.get_barrier_semaphore()
    for step in range(1, count):
        pl.semaphore_signal(barrier, inc=1, device_id={"span": lax.rem(span + step, count)}, device_id_type=MESH)
    pl.semaphore_signal(barrier, inc=1, device_id={"tensor": partner}, device_id_type=MESH)

    @pl.when(left)
    def _():
        pl.semaphore_signal(barrier, inc=1, device_id={"tensor": me - 2}, device_id_type=MESH)

    @pl.when(right)
    def _():
        pl.semaphore_signal(barrier, inc=1, device_id={"tensor": me + 2}, device_id_type=MESH)

    moves = [
        (retain_hbm, retain_ref, 0),
        (tokens_hbm, tokens_ref, 1),
        (rate_hbm, rate_ref, 2),
        (angle_hbm, angle_ref, 2),
        (input_hbm, input_ref, 2),
        (output_hbm, output_ref, 2),
        (norm_gain_hbm, norm_gain_ref, 2),
        (bias_hbm, bias_ref, 2),
        (skip_hbm, skip_ref, 2),
        (gain_hbm, gain_ref, 2),
        (weight_hbm, weight_ref.at[0], 3),
        (mixer_hbm, mixer_ref, 3),
    ]
    loads = [pltpu.make_async_copy(source, target, load_sem.at[item]) for source, target, item in moves]
    for load in loads:
        load.start()

    row = lax.broadcasted_iota(jnp.int32, (length, length), 0)
    column = lax.broadcasted_iota(jnp.int32, (length, length), 1)
    ones = group_ones(channels)
    loads[0].wait()
    diagonal = jnp.where(row == column, jnp.broadcast_to(retain_ref[...], (length, length)), 0.0)
    keep = sum(dot(piece, jnp.ones((length, LANES), jnp.bfloat16)) for piece in pieces(diagonal, 3))
    kept = keep.reshape(blocks, STEPS, LANES)
    while kept.shape[0] > 1:
        half = kept.shape[0] // 2
        kept = kept[:half] * kept[half:]
    kept = kept[0]
    for by in (1, 2, 4):
        kept = kept * pltpu.roll(kept, by, 0)
    loads[1].wait()
    tokens = tokens_ref[...]
    values = tokens.astype(jnp.float32)
    total = jnp.sum(values, axis=0, keepdims=True)
    squares = jnp.sum(values * values, axis=0, keepdims=True)
    summed = jnp.concatenate([total, squares, jnp.zeros((6, channels), jnp.float32)], axis=0)
    summed = sum(dot(piece, ones) for piece in pieces(summed, 3))
    top = lax.broadcasted_iota(jnp.int32, (8, channels), 0) < 2
    total_ref[...] = jnp.where(top, summed, wide(kept, channels))
    pl.semaphore_wait(barrier, count + left.astype(jnp.int32) + right.astype(jnp.int32))
    stats = (total_ref, totals_ref, total_send, total_recv)
    to_later(count, *stats)
    swap = remote(weight_hbm, weight_ref.at[1], weight_send, weight_recv, "tensor", partner)

    for load in loads[2:10]:
        load.wait()
    rate, angle = rate_ref[...], angle_ref[...]
    size = jnp.exp(-rate)
    turn_re = size * jnp.cos(angle)
    turn_im = size * jnp.sin(angle)
    weight = (1.0 - size) * input_ref[...]
    read_re = weight * output_ref[0]
    read_im = weight * output_ref[1]
    power_re, power_im = jnp.ones_like(rate), jnp.zeros_like(rate)
    lag_rows = []
    for lag in range(STEPS + 1):
        if lag < STEPS:
            lag_rows.append(jnp.sum(read_re * power_re - read_im * power_im, axis=0, keepdims=True))
        power_ref[0, lag] = power_re
        power_ref[1, lag] = power_im
        power_re, power_im = power_re * turn_re - power_im * turn_im, power_re * turn_im + power_im * turn_re
    unit_ref[0] = read_re * turn_re - read_im * turn_im
    unit_ref[1] = read_re * turn_im + read_im * turn_re
    whole = jnp.exp(-rate * length)
    whole_ref[0] = whole * jnp.cos(angle * length)
    whole_ref[1] = whole * jnp.sin(angle * length)
    step_row = lax.broadcasted_iota(jnp.int32, (STEPS, channels), 0)

    def table(part, carried):
        here = pl.ds(part, 1)
        re = jnp.broadcast_to(unit_ref[0, here, :], (STEPS, channels))
        im = jnp.broadcast_to(unit_ref[1, here, :], (STEPS, channels))
        for bit in (1, 2, 4):
            chosen = (step_row // bit) % 2 == 1
            by_re = jnp.where(chosen, jnp.broadcast_to(power_ref[0, bit, here, :], (STEPS, channels)), 1.0)
            by_im = jnp.where(chosen, jnp.broadcast_to(power_ref[1, bit, here, :], (STEPS, channels)), 0.0)
            re, im = re * by_re - im * by_im, re * by_im + im * by_re
        read_ref[0, part] = re
        read_ref[1, part] = im
        return carried

    lax.fori_loop(0, ndim, table, 0)

    sums = dot(tokens, ones)
    squares = sum(dot(piece, ones) for piece in pieces(values * values, 2))
    lower = (column <= row).astype(jnp.bfloat16)
    cum_sum = sum(dot(lower, piece) for piece in pieces(sums, 3))
    cum_sq = sum(dot(lower, piece) for piece in pieces(squares, 3))
    place_in = lax.broadcasted_iota(jnp.int32, (length, LANES), 0) % STEPS
    prefix = keep
    suffix = jnp.where(place_in < STEPS - 1, pltpu.roll(keep, length - 1, 0), 1.0)
    for by in (1, 2, 4):
        prefix = jnp.where(place_in >= by, prefix * pltpu.roll(prefix, by, 0), prefix)
        suffix = jnp.where(place_in + by < STEPS, suffix * pltpu.roll(suffix, length - by, 0), suffix)
    prefix_ref[...] = prefix.reshape(blocks, STEPS, LANES)
    position = lax.broadcasted_iota(jnp.int32, (length, LANES), 0)
    share = wide(1.0 / ((span * length + position + 1) * GROUP).astype(jnp.float32), channels)

    from_earlier(count, *stats)
    swap.start()
    before_ref[...] = jnp.zeros((8, channels), jnp.float32)
    for other in range(count - 1):

        @pl.when(other < span)
        def _():
            before_ref[...] += totals_ref[other]

    average = (before_ref[0:1] + cum_sum) * share
    spread = (before_ref[1:2] + cum_sq) * share - average * average
    inverse = lax.rsqrt(spread + NORM_EPS)
    normed = (values - average) * inverse * norm_gain_ref[...] + bias_ref[...]
    normed_ref[...] = normed
    scaled_ref[...] = (normed * wide(suffix, channels)).reshape(blocks, STEPS, channels)

    width = min(ENTER, channels)
    for lanes in lanes_of(channels, width):
        powers = [(power_ref[0, lag, :, lanes], power_ref[1, lag, :, lanes]) for lag in range(STEPS + 1)]

        def enter(block, carried):
            re, im = carried
            start_ref[0, block, :, lanes] = re
            start_ref[1, block, :, lanes] = im
            factor = wide(prefix_ref[block, STEPS - 1 : STEPS, :], width)
            add_re = jnp.broadcast_to(scaled_ref[block, STEPS - 1 : STEPS, lanes], (ndim, width))
            add_im = None
            for step in reversed(range(STEPS - 1)):
                entry = scaled_ref[block, step : step + 1, lanes]
                by_re, by_im = powers[STEPS - 1 - step]
                add_re = add_re + by_re * entry
                add_im = by_im * entry if add_im is None else add_im + by_im * entry
            re, im = re * factor, im * factor
            by_re, by_im = powers[STEPS]
            return by_re * re - by_im * im + add_re, by_re * im + by_im * re + add_im

        zero = jnp.zeros((ndim, width), jnp.float32)
        re, im = lax.fori_loop(0, blocks, enter, (zero, zero), unroll=UNROLL)
        state_ref[0:ndim, lanes] = re.astype(state_ref.dtype)
        state_ref[ndim : 2 * ndim, lanes] = im.astype(state_ref.dtype)
    states = (state_ref, states_ref, state_send, state_recv)
    to_later(count, *states)

    for lanes in lanes_of(channels, LANES):
        reach = jnp.where(place_in >= 0, 1.0, 0.0)
        here = normed_ref[:, lanes]
        within = here * lag_rows[0][:, lanes]
        for lag in range(1, STEPS):
            reach = jnp.where(place_in >= lag, reach * (pltpu.roll(keep, lag - 1, 0) if lag > 1 else keep), 0.0)
            within = within + pltpu.roll(here, lag, 0) * (lag_rows[lag][:, lanes] * reach)
        ema_ref[:, lanes] = within + skip_ref[:, lanes] * here

    @pl.when(end)
    def _():
        land_ref[near] = jnp.zeros(land_ref.shape[1:], land_ref.dtype)

    loads[10].wait()
    loads[11].wait()
    swap.wait_recv()
    carry_ref[...] = jnp.zeros(carry_ref.shape, jnp.float32)
    from_earlier(count, *states)
    for other in range(count - 1):

        @pl.when(other < span)
        def _():
            kept = totals_ref[other, 2:3, :]
            re, im = carry_ref[0], carry_ref[1]
            by_re, by_im = whole_ref[0], whole_ref[1]
            carry_ref[0] = (by_re * re - by_im * im) * kept + states_ref[other, 0:ndim].astype(jnp.float32)
            carry_ref[1] = (by_re * im + by_im * re) * kept + states_ref[other, ndim : 2 * ndim].astype(jnp.float32)

    width = min(LEAVE, channels)
    inside = rows // STEPS

    def produce(pair, side):
        chunk = 2 * pair + side
        for lanes in lanes_of(channels, width):
            whole_re, whole_im = power_ref[0, STEPS, :, lanes], power_ref[1, STEPS, :, lanes]
            re, im = carry_ref[0, :, lanes], carry_ref[1, :, lanes]
            for block in range(chunk * inside, (chunk + 1) * inside):
                start_ref[0, block, :, lanes] += re
                start_ref[1, block, :, lanes] += im
                factor = wide(prefix_ref[block, STEPS - 1 : STEPS, :], width)
                re, im = (whole_re * re - whole_im * im) * factor, (whole_re * im + whole_im * re) * factor
            carry_ref[0, :, lanes] = re
            carry_ref[1, :, lanes] = im
            reads = [None] * inside
            for part in range(ndim):
                by_re, by_im = read_ref[0, part, :, lanes], read_ref[1, part, :, lanes]
                for spot in range(inside):
                    block = chunk * inside + spot
                    term = by_re * start_ref[0, block, part : part + 1, lanes] - by_im * start_ref[1, block, part : part + 1, lanes]
                    reads[spot] = term if reads[spot] is None else reads[spot] + term
            for spot in range(inside):
                here = slice((chunk * inside + spot) * STEPS, (chunk * inside + spot + 1) * STEPS)
                ema_ref[here, lanes] += reads[spot] * wide(prefix_ref[chunk * inside + spot], width)
        ema = ema_ref[chunk * rows : (chunk + 1) * rows, :]
        active_ref[pair, side] = (ema / (1.0 + jnp.exp(-ema))).astype(jnp.bfloat16)

        @pl.when(core != side)
        def _():
            remote(active_ref.at[pair, side], mate_ref.at[pair], mate_send, mate_recv.at[pair], "tensor", partner).start()

    def hop(way, item, target):
        return remote(hop_ref.at[way, item], land_ref.at[way, item], hop_send.at[way], hop_recv.at[way, item], "tensor", target)

    def multiply(pair):
        remote(active_ref.at[pair, 1 - core], mate_ref.at[pair], mate_send, mate_recv.at[pair], "tensor", partner).wait_recv()
        product = dot(active_ref[pair, core], weight_ref[0]) + dot(mate_ref[pair], weight_ref[1])
        cuts = [
            product[sub * fine : (sub + 1) * fine, lanes]
            for sub in range(subs)
            for lanes in lanes_of(columns, piece_columns)
        ]
        for spot, cut in enumerate(cuts):
            part_ref[pair * subs * PARTS + spot] = cut

        @pl.when(end)
        def _():
            for spot, cut in enumerate(cuts):
                item = pair * subs * PARTS + spot
                hop_ref[near, item] = cut.astype(jnp.bfloat16)
                hop(near, item, inner).start()

    for pair in range(pairs):
        produce(pair, 0)
        produce(pair, 1)

        @pl.when(core == 0)
        def _():
            multiply(pair)

    @pl.when(core == 1)
    def _():
        for pair in range(pairs):
            multiply(pair)

    def home(item):
        slot = all_ref.at[item // subs, core, item % subs]
        return remote(slot, slot, home_send, home_recv.at[item // subs], "tensor", partner)

    def relay(item):
        @pl.when(jnp.logical_not(end))
        def _():
            hop(near, item, inner).wait_recv()
            hop_ref[near, item] = (part_ref[item] + land_ref[near, item].astype(jnp.float32)).astype(jnp.bfloat16)
            hop(near, item, inner).start()

    def close(item):
        hop(far, item, outer).wait_recv()
        running = part_ref[item] + land_ref[far, item].astype(jnp.float32)

        @pl.when(jnp.logical_not(end))
        def _():
            hop_ref[far, item] = running.astype(jnp.bfloat16)
            hop(far, item, outer).start()

        return running + land_ref[near, item].astype(jnp.float32)

    def settle(block, halves):
        squares = sum(jnp.sum(half * half, axis=1, keepdims=True) for half in halves) / columns
        scale = lax.rsqrt(squares + SCALE_EPS)
        for half, lanes in zip(halves, lanes_of(columns, piece_columns)):
            all_ref[block // subs, core, block % subs, :, lanes] = (half * scale * gain_ref[:, lanes]).astype(jnp.bfloat16)
        home(block).start()

    def arrived(pair):
        slot = all_ref.at[pair, core]
        remote(slot, slot, home_send, home_recv.at[pair], "tensor", partner).wait_recv()

    def finish(pair):
        arrived(pair)
        gathered = all_ref[pair].reshape(2 * rows, columns)
        out_ref[2 * pair * rows : 2 * (pair + 1) * rows, :] = dot(gathered, mixer_ref[...]).astype(jnp.bfloat16)

    def finish_side(pair, side):
        gathered = all_ref[pair, side].reshape(rows, columns)
        first = pl.multiple_of((2 * pair + side) * rows, rows)
        out_ref[pl.ds(first, rows), :] = dot(gathered, mixer_ref[...]).astype(jnp.bfloat16)

    held = []
    for item in range(count_of + LAG):
        if item < count_of:
            relay(item)
        item -= LAG
        if item >= 0:
            held.append(close(item))
            if len(held) == PARTS:
                block = item // PARTS
                settle(block, held)
                held = []
                if block % subs == subs - 1 and block >= subs:
                    finish(block // subs - 1)
    finish_side(pairs - 1, core)
    arrived(pairs - 1)
    finish_side(pairs - 1, 1 - core)

    sent_later(count, *stats)
    sent_later(count, *states)
    swap.wait_send()
    remote(mate_ref, mate_ref, mate_send, mate_recv.at[0], "tensor", partner).wait_send()
    remote(hop_ref.at[0], land_ref.at[0], home_send, home_recv.at[0], "tensor", partner).wait_send()
    remote(hop_ref.at[0], land_ref.at[0], hop_send.at[near], hop_recv.at[0, 0], "tensor", inner).wait_send()

    @pl.when(jnp.logical_not(end))
    def _():
        remote(hop_ref.at[0], land_ref.at[0], hop_send.at[far], hop_recv.at[0, 0], "tensor", outer).wait_send()


def layer(tokens, retain, norm_gain, norm_bias, rate, angle, source, output, skip, weight, gain, mixer):
    length, channels = tokens.shape
    ndim = rate.shape[0]
    blocks = length // STEPS
    count = lax.axis_size("span")
    chips = lax.axis_size("tensor") // 2
    columns = weight.shape[1]
    pairs = length // (2 * ROWS)
    items = PARTS * length // (2 * FINE)
    f32, bf16 = jnp.float32, jnp.bfloat16
    sems = pltpu.SemaphoreType.DMA
    hbm = pl.BlockSpec(memory_space=pltpu.HBM)
    operands = [
        tokens,
        retain.reshape(1, -1),
        norm_gain.reshape(1, -1),
        norm_bias.reshape(1, -1),
        rate,
        angle,
        source,
        output,
        skip.reshape(1, -1),
        gain.reshape(1, -1),
        weight,
        mixer,
    ]
    held = [pltpu.VMEM(a.shape, a.dtype) for a in operands[:10]]
    return pl.pallas_call(
        functools.partial(layer_kernel, count, chips),
        out_shape=pltpu.VMEM((length, mixer.shape[1]), bf16),
        in_specs=[hbm] * 12,
        out_specs=VMEM,
        scratch_shapes=held
        + [
            pltpu.VMEM((2,) + weight.shape, bf16),
            pltpu.VMEM(mixer.shape, bf16),
            pltpu.VMEM((8, channels), f32),
            pltpu.VMEM((count, 8, channels), f32),
            pltpu.VMEM((8, channels), f32),
            pltpu.VMEM((length, channels), f32),
            pltpu.VMEM((blocks, STEPS, channels), f32),
            pltpu.VMEM((blocks, STEPS, LANES), f32),
            pltpu.VMEM((2, STEPS + 1, ndim, channels), f32),
            pltpu.VMEM((2, ndim, channels), f32),
            pltpu.VMEM((2, ndim, channels), f32),
            pltpu.VMEM((2, ndim, channels), f32),
            pltpu.VMEM((2, ndim, STEPS, channels), f32),
            pltpu.VMEM((2, blocks, ndim, channels), f32),
            pltpu.VMEM((2 * ndim, channels), bf16),
            pltpu.VMEM((count, 2 * ndim, channels), bf16),
            pltpu.VMEM((length, channels), f32),
            pltpu.VMEM((pairs, 2, ROWS, channels), bf16),
            pltpu.VMEM((pairs, ROWS, channels), bf16),
            pltpu.VMEM((items, FINE, columns // PARTS), f32),
            pltpu.VMEM((2, items, FINE, columns // PARTS), bf16),
            pltpu.VMEM((2, items, FINE, columns // PARTS), bf16),
            pltpu.VMEM((pairs, 2, ROWS // FINE, FINE, columns), bf16),
            sems((4,)),
            sems(()),
            sems(()),
            sems(()),
            sems(()),
            sems(()),
            sems(()),
            sems(()),
            sems((pairs,)),
            sems((2,)),
            sems((2, items)),
            sems(()),
            sems((pairs,)),
        ],
        compiler_params=pltpu.CompilerParams(collective_id=0, has_side_effects=True),
        name="layer",
    )(*operands)


def solution(mesh):
    in_specs = (
        P("span", "tensor"),
        P("span"),
        P("tensor"),
        P("tensor"),
        P(None, "tensor"),
        P(None, "tensor"),
        P(None, "tensor"),
        P(None, None, "tensor"),
        P("tensor"),
        P("tensor", None),
        P(),
        P(None, "tensor"),
    )
    return jax.shard_map(layer, mesh=mesh, in_specs=in_specs, out_specs=P("span", "tensor"), check_vma=False)
```
